128 devices in a mesh: space: 16 (over y, z_hi, core), chaos: 8 (over x, z_lo).
Axes of the slice: x: 4, y: 4, z: 4 (z_hi: 2, z_lo: 2; z = z_hi * 2 + z_lo), core: 2. Of those that a mesh axis runs over, the one named last changes fastest.
Arguments:
- forcing: float32 [288, 256, 128], P('chaos', 'space'), may hold values from -12 to 12, as said below
- start_guess: float32 [288, 256, 128], P('chaos', 'space'), may hold values from -2 to 2, as said below
- mean_field: float32 [256, 128], P('space'), may hold values from 1 to 2
- mode_fields: float32 [10, 256, 128], P(None, 'space'), may hold values from -0.04 to 0.04
- multi_index: int32 [288, 10], P('chaos'), may hold values from -1 to 3, as said below
- coupled_slot: int32 [288, 20], P('chaos'), may hold values from 0 to 288, as said below
Outputs:
- approximation: float32 [288, 256, 128], P('chaos', 'space')
- recursive_residual: float32 [288, 256, 128], P('chaos', 'space')
The draws below stay inside these ranges and needn't reach their ends.
Inputs may be any that keep to these rules, and one draw needn't show every extreme that they name: `multi_index`: row s is the multi-index of the chaos term placed in slot s: 10 nonnegative entries summing to at most 3, each such multi-index in exactly one slot; the slots without a term hold -1 in every entry. `coupled_slot`: entry (s, k) for k < 10 is the slot whose multi-index is that of slot s with one more in mode k, entry (s, 10 + k) the slot with one less in mode k; 288 where no such term exists or slot s holds no term. `forcing`: zero in the slots that hold no term. `start_guess`: zero in the slots that hold no term.
All inputs are finite; a program needn't handle non-finite values.
Results may differ from the reference program's by a relative error of at most 0.0003.
Values sent between devices are 32-bit elements; how exact they have to be, the bound alone decides.
A program may use at most 128 MiB of HBM per device.

```python
import math
import jax
import jax.numpy as jnp
import numpy as np

MODES = 10
DEGREE = 3
TERMS = 286
SLOTS = 288
ROWS = 128
COLUMNS = 256
ITERS = 2


def build_indices(mode_count, remaining):
    if mode_count == 0:
        return [[]]
    listed = []
    for leading in range(remaining + 1):
        for tail_part in build_indices(mode_count - 1, remaining - leading):
            listed.append([leading] + tail_part)
    return listed


def term_tables(mode_count, degree_most):
    listed = sorted(build_indices(mode_count, degree_most), key=sum)
    lookup = {}
    for position, entry in enumerate(listed):
        lookup[tuple(entry)] = position
    term_count = len(listed)
    raising = np.full((term_count, mode_count), term_count, np.int32)
    lowering = np.full((term_count, mode_count), term_count, np.int32)
    for position, entry in enumerate(listed):
        for kl_mode in range(mode_count):
            higher = list(entry)
            higher[kl_mode] = higher[kl_mode] + 1
            raising[position, kl_mode] = lookup.get(tuple(higher), term_count)
            if entry[kl_mode] > 0:
                lowered_entry = list(entry)
                lowered_entry[kl_mode] = lowered_entry[kl_mode] - 1
                lowering[position, kl_mode] = lookup[tuple(lowered_entry)]
    return (np.array(listed, np.int32), raising, lowering)


def slot_layout(key):
    term_table, raising, lowering = term_tables(MODES, DEGREE)
    holder = jax.random.permutation(jax.random.fold_in(key, 11), SLOTS).astype(jnp.int32)
    slot_of = jnp.argsort(holder, stable=True).astype(jnp.int32)
    slot_ext = jnp.concatenate([slot_of[:TERMS], jnp.full((1,), SLOTS, jnp.int32)])
    living = holder < TERMS
    clipped = jnp.minimum(holder, TERMS - 1)
    multi_rows = jnp.where(living[:, None], jnp.asarray(term_table)[clipped], -1).astype(jnp.int32)
    raised = slot_ext[jnp.asarray(raising)[clipped]]
    lowered = slot_ext[jnp.asarray(lowering)[clipped]]
    coupled = jnp.where(living[:, None], jnp.concatenate([raised, lowered], axis=1), SLOTS).astype(jnp.int32)
    return (multi_rows, coupled, living)


def draw_multi_index(key, part):
    return slot_layout(key)[0]


def draw_coupled_slot(key, part):
    return slot_layout(key)[1]


def draw_forcing(key, part):
    living = slot_layout(key)[2]
    noise_key = jax.random.fold_in(key, 23)
    columns = jnp.arange(COLUMNS, dtype=jnp.float32)[None, :, None] / COLUMNS
    slotted = jnp.arange(SLOTS, dtype=jnp.float32)[:, None, None] / SLOTS
    scaling = jnp.exp(jnp.log(3.0) * (columns + slotted)) / 3.0
    values = jnp.clip(jax.random.normal(noise_key, (SLOTS, COLUMNS, ROWS), jnp.float32), -4.0, 4.0) * scaling
    return jnp.where(living[:, None, None], values, 0.0)


def draw_start_guess(key, part):
    living = slot_layout(key)[2]
    noise_key = jax.random.fold_in(key, 29)
    values = 0.5 * jnp.clip(jax.random.normal(noise_key, (SLOTS, COLUMNS, ROWS), jnp.float32), -4.0, 4.0)
    return jnp.where(living[:, None, None], values, 0.0)


def shard_levels(stream_key, shape, pieces, smallest, top_value):
    factor_of = 1.0
    for dim, parts in pieces:
        steps = jax.random.uniform(jax.random.fold_in(jax.random.fold_in(stream_key, 6), dim), (parts,), jnp.float32, smallest / len(pieces), top_value / len(pieces))
        factor_of = factor_of * jnp.repeat(jnp.exp(steps), shape[dim] // parts).reshape((-1,) + (1,) * (len(shape) - 1 - dim))
    return factor_of


def setup_inputs(seed: int = 0) -> dict:
    keys = jax.random.split(jax.random.key(seed), 7)
    forcing = draw_forcing(jax.random.fold_in(keys[6], 71), 0)
    start_guess = draw_start_guess(jax.random.fold_in(keys[6], 71), 0)
    mean_field = jnp.clip(jnp.exp(math.log(2.0) - 0.6931472 * jax.random.uniform(keys[2], (COLUMNS, ROWS), jnp.float32) ** shard_levels(keys[2], (COLUMNS, ROWS), ((0, 16),), -0.2, 0.2)), 1.0, 2.0)
    mode_fields = jnp.clip(jax.random.uniform(keys[3], (MODES, COLUMNS, ROWS), jnp.float32, -0.04, 0.04) * shard_levels(keys[3], (MODES, COLUMNS, ROWS), ((1, 16),), -0.4, 0.0), -0.04, 0.04)
    multi_index = draw_multi_index(jax.random.fold_in(keys[6], 71), 0)
    coupled_slot = draw_coupled_slot(jax.random.fold_in(keys[6], 71), 0)
    return dict(forcing=forcing, start_guess=start_guess, mean_field=mean_field, mode_fields=mode_fields, multi_index=multi_index, coupled_slot=coupled_slot)


def stencil(values, coeffs):
    col_faces = 0.5 * (coeffs[1:] + coeffs[:-1])
    col_flux = col_faces * (values[:, 1:] - values[:, :-1])
    across = col_flux[:, :-1] - col_flux[:, 1:]
    inner_coef = jnp.pad(coeffs[1:-1], ((0, 0), (1, 1)))
    inner_vals = jnp.pad(values[:, 1:-1], ((0, 0), (0, 0), (1, 1)))
    row_faces = 0.5 * (inner_coef[:, 1:] + inner_coef[:, :-1])
    row_flux = row_faces * (inner_vals[:, :, 1:] - inner_vals[:, :, :-1])
    return across + row_flux[:, :, :-1] - row_flux[:, :, 1:]

def coupling(multi_index, coupled_slot, slot_count, mode_count):
    degrees = multi_index.astype(jnp.float32)
    raise_weight = jnp.where(coupled_slot[:, :mode_count] < slot_count, jnp.sqrt(degrees + 1.0), 0.0)
    lower_weight = jnp.sqrt(jnp.maximum(degrees, 0.0))
    raise_index = jnp.minimum(coupled_slot[:, :mode_count], slot_count - 1).astype(jnp.int32)
    lower_index = jnp.minimum(coupled_slot[:, mode_count:], slot_count - 1).astype(jnp.int32)
    return (raise_weight, lower_weight, raise_index, lower_index)

def operate(term_field, coeff_ext, raise_weight, lower_weight, raise_index, lower_index):
    extended = jnp.pad(term_field, ((0, 0), (1, 1), (0, 0)))
    result = stencil(extended, coeff_ext[0])
    for kl_mode in range(MODES):
        mixture = raise_weight[:, kl_mode, None, None] * extended[raise_index[:, kl_mode]]
        mixture = mixture + lower_weight[:, kl_mode, None, None] * extended[lower_index[:, kl_mode]]
        result = result + stencil(mixture, coeff_ext[kl_mode + 1])
    return result

def reference(forcing, start_guess, mean_field, mode_fields, multi_index, coupled_slot):
    raise_weight, lower_weight, raise_index, lower_index = coupling(multi_index, coupled_slot, SLOTS, MODES)
    stacked = jnp.concatenate([mean_field[None], mode_fields], axis=0)
    coeff_ext = jnp.pad(stacked, ((0, 0), (1, 1), (0, 0)))

    def apply_op(term_field):
        return operate(term_field, coeff_ext, raise_weight, lower_weight, raise_index, lower_index)
    approximation = start_guess
    residual = forcing - apply_op(start_guess)
    direction = residual
    norm_now = jnp.sum(residual * residual)
    for number in range(ITERS):
        applied = apply_op(direction)
        step_length = norm_now / jnp.sum(direction * applied)
        approximation = approximation + step_length * direction
        residual = residual - step_length * applied
        if number + 1 < ITERS:
            norm_next = jnp.sum(residual * residual)
            direction = residual + norm_next / norm_now * direction
            norm_now = norm_next
    return (approximation, residual)
```

```python
import functools
import math

import jax
import jax.numpy as jnp
import numpy as np
from jax import lax
from jax.experimental import pallas as pl
from jax.experimental.pallas import tpu as pltpu
from jax.sharding import PartitionSpec as P

MESH = pl.DeviceIdType.MESH
F32 = jnp.float32
DEGREE = 3
LANES = 128
PAD = 40


def term_list(modes, degree):
    def build(count, left):
        if count == 0:
            return [()]
        return [(a,) + tail for a in range(left + 1) for tail in build(count - 1, left - a)]

    return sorted(build(modes, degree), key=sum)


def code_of(term):
    return sum(m * 4**k for k, m in enumerate(term))


def kernel(
    cfg,
    f_ref,
    x_ref,
    mean_ref,
    modes_ref,
    index_ref,
    code_ref,
    xo_ref,
    ro_ref,
    sbx,
    sbf,
    scode,
    scoef,
    rx,
    rf,
    rcode,
    rcoef,
    pick,
    field,
    forced,
    halo,
    grad,
    flux,
    faces,
    outs,
    back,
    dot_local,
    dot_a,
    dot_b_local,
    dot_b,
    sx,
    sf,
    sc,
    sk,
    sh,
    so,
    sda,
    sdb,
    qx,
    qf,
    qc,
    qk,
    qh,
    qo,
    qda,
    qdb,
):
    slots, cols, terms, modes = cfg["slots"], cfg["cols"], cfg["terms"], cfg["modes"]
    rows = cfg["rows"]
    full = cfg["full"]
    position = {t: i for i, t in enumerate(terms)}

    space, chaos = lax.axis_index("space"), lax.axis_index("chaos")
    pair, core = space // 2, space % 2
    xx, zz = chaos // 2, chaos % 2
    lane_at = xx + zz * (3 - 2 * xx)
    member = 8 * zz + 2 * lane_at + core
    me = 16 * pair + member
    last = 127

    def device(j):
        p = (j // 2) % 8
        z = p // 4
        inner = p % 4
        x = inner + z * (3 - 2 * inner)
        return (2 * (j // 16) + j % 2, 2 * x + z)

    def remote(src, dst, ssem, rsem, where):
        return pltpu.make_async_remote_copy(
            src_ref=src, dst_ref=dst, send_sem=ssem, recv_sem=rsem, device_id=where, device_id_type=MESH
        )

    barrier = pltpu.get_barrier_semaphore()

    def greet(j):
        pl.semaphore_signal(barrier, inc=1, device_id=device(j), device_id_type=MESH)

    for o in range(1, 16):
        greet(16 * pair + (member + o) % 16)
    for o in range(1, 8):
        greet(16 * ((pair + o) % 8) + member)
    pl.when(me > 0)(lambda: greet(me - 1))
    pl.when(me < last)(lambda: greet(me + 1))

    zero8 = jnp.zeros((8, LANES), F32)
    for c in range(cols):
        for src, dst in ((x_ref, sbx), (f_ref, sbf)):
            dst[c, 32:40, :] = zero8
            dst[c, 0:slots, :] = src[pl.ds(c, slots, stride=cols), :]
    power = jnp.left_shift(1, 2 * lax.broadcasted_iota(jnp.int32, (1, modes), 1)).astype(F32)
    code = jnp.sum(index_ref[...].astype(F32) * power, axis=1, keepdims=True)
    at_sub = lax.broadcasted_iota(jnp.int32, (slots, LANES), 0)
    at_lane = lax.broadcasted_iota(jnp.int32, (slots, LANES), 1)
    row = jnp.sum(jnp.where(at_sub == at_lane, code, 0.0), axis=0, keepdims=True)
    lane1 = lax.broadcasted_iota(jnp.int32, (1, LANES), 1)
    row = jnp.where(lane1 < slots, row, -1.0)
    scode[...] = jnp.broadcast_to(row, (8, LANES))

    mine = 2 * lane_at + core
    other = 2 * lane_at + (1 - core)
    for which, first in ((0, 2 * mine), (1, 2 * other)):
        for c in range(2):
            scoef[which, c, 8:16, :] = zero8
            scoef[which, c, 0:1, :] = mean_ref[pl.ds(first + c, 1), :]
            for k in range(modes):
                scoef[which, c, 1 + k : 2 + k, :] = modes_ref[k, pl.ds(first + c, 1), :]

    @pl.when(me == 0)
    def _():
        for i in range(3):
            halo[i, 0] = jnp.zeros((full, LANES), F32)

    @pl.when(me == last)
    def _():
        for i in range(3):
            halo[i, 1] = jnp.zeros((full, LANES), F32)

    greeted = 15 + 7 + jnp.where(me > 0, 1, 0) + jnp.where(me < last, 1, 0)
    pl.semaphore_wait(barrier, greeted)

    def piece(send, land, ssem, rsem, i):
        where = device(8 * space + i)
        return remote(send, land, ssem.at[i], rsem.at[chaos], where)

    def scatter(copy_of, keep):
        for o in range(8):
            i = (o + chaos) % 8
            target = 8 * space + i
            pl.when(target != me)(lambda: copy_of(i).start())
            pl.when(target == me)(lambda: keep(i))

    own_source = (me // 8) == space

    def arrive(copy_of):
        for g in range(8):
            here = jnp.logical_and(own_source, chaos == g)
            pl.when(jnp.logical_not(here))(lambda: copy_of(g).wait_recv())

    def code_copy(i):
        return piece(scode, rcode.at[chaos], sc, qc, i)

    def x_copy(i):
        return piece(sbx.at[pl.ds(2 * i, 2)], rx.at[chaos], sx, qx, i)

    def f_copy(i):
        return piece(sbf.at[pl.ds(2 * i, 2)], rf.at[chaos], sf, qf, i)

    def keep_code(i):
        rcode[chaos] = scode[...]

    def keep_x(i):
        rx[chaos] = sbx[pl.ds(2 * i, 2)]

    def keep_f(i):
        rf[chaos] = sbf[pl.ds(2 * i, 2)]

    sibling = me + 1 - 2 * core
    coef_copy = remote(scoef.at[1], rcoef, sk, qk, device(sibling))
    scatter(code_copy, keep_code)
    coef_copy.start()
    scatter(x_copy, keep_x)
    scatter(f_copy, keep_f)

    def code_wait(g):
        return remote(scode, rcode.at[g], sc.at[0], qc.at[g], device(me))

    def x_wait(g):
        return remote(sbx.at[0:2], rx.at[g], sx.at[0], qx.at[g], device(me))

    def f_wait(g):
        return remote(sbf.at[0:2], rf.at[g], sf.at[0], qf.at[g], device(me))

    arrive(code_wait)
    sub40 = lax.broadcasted_iota(jnp.int32, (PAD, LANES), 0)
    lane40 = lax.broadcasted_iota(jnp.int32, (PAD, LANES), 1)
    for g in range(8):
        spread = jnp.where(sub40 == lane40, rcode[g, 0:1, :], 0.0)
        placed = jnp.sum(spread, axis=1, keepdims=True)
        pick[PAD * g : PAD * (g + 1), :] = jnp.where(placed == code_ref[0:1, :], 1.0, 0.0)

    def parts(value):
        high = value.astype(jnp.bfloat16)
        rest = value - high.astype(F32)
        mid = rest.astype(jnp.bfloat16)
        low = (rest - mid.astype(F32)).astype(jnp.bfloat16)
        return [high, mid, low]

    def select(first, second, transposed):
        both = parts(first) + parts(second)
        return lax.dot_general(
            pick[...].astype(jnp.bfloat16),
            jnp.concatenate(both, axis=1),
            (((0 if transposed else 1,), (0,)), ((), ())),
            preferred_element_type=F32,
        )

    def column(result, c):
        base = 3 * LANES * c
        return (
            result[:, base : base + LANES]
            + result[:, base + LANES : base + 2 * LANES]
            + result[:, base + 2 * LANES : base + 3 * LANES]
        )

    coef_copy.wait_recv()
    local = core == zz
    for c in range(2):
        field[0, c, rows:full, :] = jnp.where(local, scoef[0, c], rcoef[c])

    arrive(x_wait)
    got = select(rx[:, 0].reshape(8 * PAD, LANES), rx[:, 1].reshape(8 * PAD, LANES), True)
    for c in range(2):
        field[0, c, 0:rows, :] = column(got, c)[0:rows]

    def halo_left(i):
        return remote(field.at[i, 0], halo.at[i, 1], sh.at[i, 0], qh.at[i, 1], device(me - 1))

    def halo_right(i):
        return remote(field.at[i, 1], halo.at[i, 0], sh.at[i, 1], qh.at[i, 0], device(me + 1))

    def halo_start(i):
        pl.when(me > 0)(lambda: halo_left(i).start())
        pl.when(me < last)(lambda: halo_right(i).start())

    def halo_wait(i):
        pl.when(me > 0)(lambda: halo_right(i).wait_recv())
        pl.when(me < last)(lambda: halo_left(i).wait_recv())

    halo_start(0)

    arrive(f_wait)
    got = select(rf[:, 0].reshape(8 * PAD, LANES), rf[:, 1].reshape(8 * PAD, LANES), True)
    for c in range(2):
        forced[c] = column(got, c)[0:rows]

    lane8 = lax.broadcasted_iota(jnp.int32, (8, LANES), 1)

    def back_copy(i, g):
        return remote(
            outs.at[i, g],
            back.at[i, pl.ds(2 * (me % 8), 2)],
            so.at[i, g],
            qo.at[i, me % 8],
            (me // 8, g),
        )

    def back_wait(i, j):
        return remote(outs.at[i, 0], back.at[i, pl.ds(2 * j, 2)], so.at[i, 0], qo.at[i, j], (space, chaos))

    def send_back(i):
        got = select(field[i + 1, 0, 0:rows, :], field[i + 1, 1, 0:rows, :], False)
        for c in range(2):
            whole = column(got, c)
            for g in range(8):
                outs[i, g, c] = whole[PAD * g : PAD * (g + 1)]
        for o in range(8):
            g = (o + chaos) % 8
            here = jnp.logical_and(own_source, g == chaos)
            pl.when(jnp.logical_not(here))(lambda: back_copy(i, g).start())

            @pl.when(here)
            def _():
                back[i, pl.ds(2 * (me % 8), 2)] = outs[i, g]

    def dots(which, values):
        dot_local[which] = zero8
        for n, value in enumerate(values):
            dot_local[which, n : n + 1, :] = jnp.sum(value, axis=0, keepdims=True)

    def dot_a_copy(which, o):
        return remote(
            dot_local.at[which],
            dot_a.at[which, member],
            sda.at[which, o],
            qda.at[which, member],
            device(16 * pair + (member + o) % 16),
        )

    def dot_b_copy(which, o):
        return remote(
            dot_b_local.at[which],
            dot_b.at[which, pair],
            sdb.at[which, o],
            qdb.at[which, pair],
            device(16 * ((pair + o) % 8) + member),
        )

    def dot_a_start(which):
        for o in range(1, 16):
            dot_a_copy(which, o).start()
        dot_a[which, member] = dot_local[which]

    def dot_b_start(which):
        for o in range(1, 16):
            m = (member + o) % 16
            remote(
                dot_local.at[which], dot_a.at[which, m], sda.at[which, 0], qda.at[which, m], device(me)
            ).wait_recv()
        total = dot_a[which, 0]
        for m in range(1, 16):
            total = total + dot_a[which, m]
        dot_b_local[which] = total
        for o in range(1, 8):
            dot_b_copy(which, o).start()
        dot_b[which, pair] = total

    def dot_total(which):
        for o in range(1, 8):
            m = (pair + o) % 8
            remote(
                dot_b_local.at[which], dot_b.at[which, m], sdb.at[which, 0], qdb.at[which, m], device(me)
            ).wait_recv()
        total = dot_b[which, 0]
        for m in range(1, 8):
            total = total + dot_b[which, m]
        return jnp.sum(total, axis=1, keepdims=True)

    def chunk_sum(first, second):
        return jnp.sum((first * second).reshape(-1, 8, LANES), axis=0)

    def apply(i, carry):
        halo_wait(i)

        @pl.when(i == 0)
        def _():
            for h in range(2):
                part = pl.ds(rows + 8 * h, 8)
                left, c0, c1, right = halo[0, 0, part], field[0, 0, part], field[0, 1, part], halo[0, 1, part]

                def up(value):
                    return jnp.where(lane8 < LANES - 1, pltpu.roll(value, LANES - 1, 1), 0.0)

                kinds = [
                    0.5 * (left + c0),
                    0.5 * (c0 + c1),
                    0.5 * (c1 + right),
                    0.5 * (c0 + up(c0)),
                    0.5 * (c1 + up(c1)),
                    jnp.where(lane8 == 0, 0.5 * c0, 0.0),
                    jnp.where(lane8 == 0, 0.5 * c1, 0.0),
                    zero8,
                ]
                for n, kind in enumerate(kinds):
                    faces[pl.ds(64 * h + n, 8, stride=8), :] = kind

        def gradients(b, carry):
            part = pl.ds(pl.multiple_of(8 * b, 8), 8)
            left, u0, u1, right = halo[i, 0, part], field[i, 0, part], field[i, 1, part], halo[i, 1, part]
            up0 = jnp.where(lane8 < LANES - 1, pltpu.roll(u0, LANES - 1, 1), 0.0)
            up1 = jnp.where(lane8 < LANES - 1, pltpu.roll(u1, LANES - 1, 1), 0.0)
            kinds = [u0 - left, u1 - u0, right - u1, up0 - u0, up1 - u1]
            kinds += [jnp.where(lane8 == 0, u0, 0.0), jnp.where(lane8 == 0, u1, 0.0), zero8]
            for n, kind in enumerate(kinds):
                grad[pl.ds(64 * b + n, 8, stride=8), :] = kind
            return carry

        lax.fori_loop(0, rows // 8, gradients, 0, unroll=4)

        weight = [faces[8 * k : 8 * (k + 1), :] for k in range(modes + 1)]
        for s, term in enumerate(terms):
            total = weight[0] * grad[8 * s : 8 * (s + 1), :]
            for k in range(modes):
                mix = None
                for step, square in ((1, term[k] + 1), (-1, term[k])):
                    near = term[:k] + (term[k] + step,) + term[k + 1 :]
                    if near not in position:
                        continue
                    at = position[near]
                    value = grad[8 * at : 8 * (at + 1), :]
                    if square > 1:
                        value = math.sqrt(square) * value
                    mix = value if mix is None else mix + value
                if mix is not None:
                    total = total + weight[k + 1] * mix
            flux[8 * s : 8 * (s + 1), :] = total
        for s in range(len(terms), rows):
            flux[8 * s : 8 * (s + 1), :] = zero8

        def divergence(b, carry):
            kind = [flux[pl.ds(64 * b + n, 8, stride=8), :] for n in range(7)]
            part = pl.ds(pl.multiple_of(8 * b, 8), 8)
            for c in range(2):
                down = jnp.where(lane8 > 0, pltpu.roll(kind[3 + c], 1, 1), kind[5 + c])
                value = kind[c] - kind[c + 1] + down - kind[3 + c]
                field[i + 1, c, part, :] = jnp.where(i == 0, forced[c, part, :] - value, value)
            return carry

        lax.fori_loop(0, rows // 8, divergence, 0, unroll=4)
        pl.when(i < 2)(lambda: halo_start(i + 1))
        send_back(i)

        @pl.when(i == 1)
        def _():
            r, w = field[1, :, 0:rows, :], field[2, :, 0:rows, :]
            dots(0, [chunk_sum(r, r), chunk_sum(r, w)])
            dot_a_start(0)

        return carry

    lax.fori_loop(0, 3, apply, 0)

    dot_b_start(0)
    sums = dot_total(0)
    rr, rw = sums[0:1], sums[1:2]
    alpha = rr / rw
    r0, w, v = field[1, :, 0:rows, :], field[2, :, 0:rows, :], field[3, :, 0:rows, :]
    r1 = r0 - alpha * w
    ar1 = w - alpha * v
    dots(1, [chunk_sum(r1, r1), chunk_sum(r1, ar1), chunk_sum(r1, w) + chunk_sum(r0, ar1)])
    dot_a_start(1)
    dot_b_start(1)
    sums = dot_total(1)
    rr1 = sums[0:1]
    beta = rr1 / rr
    step = rr1 / (sums[1:2] + beta * sums[2:3] + beta * beta * rw)

    for j in range(8):
        here = jnp.logical_and(own_source, me % 8 == j)
        for i in range(3):
            pl.when(jnp.logical_not(here))(lambda: back_wait(i, j).wait_recv())

    for c in range(cols):
        r0, w, v = back[0, c, 0:slots], back[1, c, 0:slots], back[2, c, 0:slots]
        x = x_ref[pl.ds(c, slots, stride=cols), :]
        xo_ref[pl.ds(c, slots, stride=cols), :] = x + (alpha + step + step * beta) * r0 - (step * alpha) * w
        r1 = r0 - alpha * w
        ro_ref[pl.ds(c, slots, stride=cols), :] = r1 - step * (w - alpha * v + beta * w)

    for i in range(8):
        target = 8 * space + i

        @pl.when(target != me)
        def _():
            code_copy(i).wait_send()
            x_copy(i).wait_send()
            f_copy(i).wait_send()

    coef_copy.wait_send()
    for i in range(3):
        pl.when(me > 0)(lambda: halo_left(i).wait_send())
        pl.when(me < last)(lambda: halo_right(i).wait_send())
        for g in range(8):
            here = jnp.logical_and(own_source, chaos == g)
            pl.when(jnp.logical_not(here))(lambda: back_copy(i, g).wait_send())
    for which in range(2):
        for o in range(1, 16):
            dot_a_copy(which, o).wait_send()
        for o in range(1, 8):
            dot_b_copy(which, o).wait_send()


def per_device(forcing, start_guess, mean_field, mode_fields, multi_index, coupled_slot):
    slots, cols, lanes = forcing.shape
    modes = mode_fields.shape[0]
    terms = term_list(modes, DEGREE)
    rows = -(-len(terms) // 8) * 8
    full = rows + 16
    wide = rows
    codes = np.full((8, wide), -2.0, np.float32)
    codes[:, : len(terms)] = [code_of(t) for t in terms]
    cfg = dict(slots=slots, cols=cols, terms=terms, modes=modes, rows=rows, full=full)
    flat = jax.ShapeDtypeStruct((slots * cols, lanes), F32)
    vmem = pl.BlockSpec(memory_space=pltpu.VMEM)
    dma, V = pltpu.SemaphoreType.DMA, pltpu.VMEM
    scratch = [
        V((cols, PAD, lanes), F32),
        V((cols, PAD, lanes), F32),
        V((8, lanes), F32),
        V((2, 2, 16, lanes), F32),
        V((8, 2, PAD, lanes), F32),
        V((8, 2, PAD, lanes), F32),
        V((8, 8, lanes), F32),
        V((2, 16, lanes), F32),
        V((8 * PAD, wide), F32),
        V((4, 2, full, lanes), F32),
        V((2, rows, lanes), F32),
        V((3, 2, full, lanes), F32),
        V((8 * rows, lanes), F32),
        V((8 * rows, lanes), F32),
        V((128, lanes), F32),
        V((3, 8, 2, PAD, lanes), F32),
        V((3, cols, PAD, lanes), F32),
        V((2, 8, lanes), F32),
        V((2, 16, 8, lanes), F32),
        V((2, 8, lanes), F32),
        V((2, 8, 8, lanes), F32),
        dma((8,)),
        dma((8,)),
        dma((8,)),
        dma,
        dma((3, 2)),
        dma((3, 8)),
        dma((2, 16)),
        dma((2, 8)),
        dma((8,)),
        dma((8,)),
        dma((8,)),
        dma,
        dma((3, 2)),
        dma((3, 8)),
        dma((2, 16)),
        dma((2, 8)),
    ]
    x, r = pl.pallas_call(
        functools.partial(kernel, cfg),
        out_shape=(flat, flat),
        in_specs=[vmem] * 6,
        out_specs=(vmem, vmem),
        scratch_shapes=scratch,
        compiler_params=pltpu.CompilerParams(
            collective_id=0, has_side_effects=True, vmem_limit_bytes=48 * 2**20
        ),
    )(
        forcing.reshape(slots * cols, lanes),
        start_guess.reshape(slots * cols, lanes),
        mean_field,
        mode_fields,
        multi_index,
        jnp.asarray(codes),
    )
    return (x.reshape(slots, cols, lanes), r.reshape(slots, cols, lanes))


def solution(mesh):
    placed = (
        P("chaos", "space", None),
        P("chaos", "space", None),
        P("space", None),
        P(None, "space", None),
        P("chaos", None),
        P("chaos", None),
    )
    return jax.shard_map(
        per_device,
        mesh=mesh,
        in_specs=placed,
        out_specs=(P("chaos", "space", None), P("chaos", "space", None)),
        check_vma=False,
    )
```

```python
import functools
import math

import jax
import jax.numpy as jnp
import numpy as np
from jax import lax
from jax.experimental import pallas as pl
from jax.experimental.pallas import tpu as pltpu
from jax.sharding import PartitionSpec as P

MESH = pl.DeviceIdType.MESH
F32 = jnp.float32
DEGREE = 3
LANES = 128
PAD = 40


def term_list(modes, degree):
    def build(count, left):
        if count == 0:
            return [()]
        return [(a,) + tail for a in range(left + 1) for tail in build(count - 1, left - a)]

    return sorted(build(modes, degree), key=sum)


def code_of(term):
    return sum(m * 4**k for k, m in enumerate(term))


def kernel(
    cfg,
    f_hbm,
    x_hbm,
    mean_hbm,
    modes_hbm,
    index_hbm,
    code_hbm,
    xo_ref,
    ro_ref,
    f_ref,
    x_ref,
    mean_ref,
    modes_ref,
    index_ref,
    code_ref,
    si,
    sbx,
    sbf,
    scode,
    scoef,
    rx,
    rf,
    rcode,
    rcoef,
    pick,
    field,
    forced,
    halo,
    grad,
    flux,
    faces,
    outs,
    back,
    dot_local,
    dot_a,
    dot_b_local,
    dot_b,
    sx,
    sf,
    sc,
    sk,
    sh,
    so,
    sda,
    sdb,
    qx,
    qf,
    qc,
    qk,
    qh,
    qo,
    qda,
    qdb,
):
    slots, cols, terms, modes = cfg["slots"], cfg["cols"], cfg["terms"], cfg["modes"]
    rows = cfg["rows"]
    full = cfg["full"]
    position = {t: i for i, t in enumerate(terms)}

    space, chaos = lax.axis_index("space"), lax.axis_index("chaos")
    pair, core = space // 2, space % 2
    xx, zz = chaos // 2, chaos % 2
    lane_at = xx + zz * (3 - 2 * xx)
    member = 8 * zz + 2 * lane_at + core
    me = 16 * pair + member
    last = 127

    def device(j):
        p = (j // 2) % 8
        z = p // 4
        inner = p % 4
        x = inner + z * (3 - 2 * inner)
        return (2 * (j // 16) + j % 2, 2 * x + z)

    def remote(src, dst, ssem, rsem, where):
        return pltpu.make_async_remote_copy(
            src_ref=src, dst_ref=dst, send_sem=ssem, recv_sem=rsem, device_id=where, device_id_type=MESH
        )

    loads = [
        pltpu.make_async_copy(src, dst, si.at[n])
        for n, (src, dst) in enumerate(
            (
                (index_hbm, index_ref),
                (x_hbm, x_ref),
                (mean_hbm, mean_ref),
                (modes_hbm, modes_ref),
                (code_hbm, code_ref),
                (f_hbm, f_ref),
            )
        )
    ]
    for load in loads:
        load.start()

    zero8 = jnp.zeros((8, LANES), F32)
    for g in range(8):
        for c in range(2):
            rx[g, c, 32:40, :] = zero8
            rf[g, c, 32:40, :] = zero8

    @pl.when(me == 0)
    def _():
        for i in range(3):
            halo[i, 0] = jnp.zeros((full, LANES), F32)

    @pl.when(me == last)
    def _():
        for i in range(3):
            halo[i, 1] = jnp.zeros((full, LANES), F32)

    barrier = pltpu.get_barrier_semaphore()

    def greet(j):
        pl.semaphore_signal(barrier, inc=1, device_id=device(j), device_id_type=MESH)

    for o in range(1, 8):
        greet(16 * ((pair + o) % 8) + member)
    for o in range(1, 16):
        greet(16 * pair + (member + o) % 16)
    pl.when(me > 0)(lambda: greet(me - 1))
    pl.when(me < last)(lambda: greet(me + 1))

    loads[0].wait()
    power = jnp.left_shift(1, 2 * lax.broadcasted_iota(jnp.int32, (modes, slots), 0)).astype(F32)
    code = jnp.sum(index_ref[...].astype(F32) * power, axis=0, keepdims=True)
    scode[...] = jnp.full((8, LANES), -1.0, F32)
    scode[:, 0:slots] = jnp.broadcast_to(code, (8, slots))

    loads[2].wait()
    loads[3].wait()
    mine = 2 * lane_at + core
    other = 2 * lane_at + (1 - core)
    for which, first in ((0, 2 * mine), (1, 2 * other)):
        for c in range(2):
            scoef[which, c, 8:16, :] = zero8
            scoef[which, c, 0:1, :] = mean_ref[pl.ds(first + c, 1), :]
            for k in range(modes):
                scoef[which, c, 1 + k : 2 + k, :] = modes_ref[k, pl.ds(first + c, 1), :]

    loads[1].wait()
    greeted = 15 + 7 + jnp.where(me > 0, 1, 0) + jnp.where(me < last, 1, 0)
    pl.semaphore_wait(barrier, greeted)

    def piece(send, land, ssem, rsem, i):
        where = device(8 * space + i)
        return remote(send, land, ssem.at[i], rsem.at[chaos], where)

    def scatter(copy_of, keep, ready=None):
        for o in range(8):
            i = (o + chaos) % 8
            target = 8 * space + i
            if ready is not None:
                ready(i)
            pl.when(target != me)(lambda: copy_of(i).start())
            pl.when(target == me)(lambda: keep(i))

    def sent(copy_of):
        for i in range(8):
            target = 8 * space + i
            pl.when(target != me)(lambda: copy_of(i).wait_send())

    own_source = (me // 8) == space

    def arrive(copy_of):
        for g in range(8):
            here = jnp.logical_and(own_source, chaos == g)
            pl.when(jnp.logical_not(here))(lambda: copy_of(g).wait_recv())

    def code_copy(i):
        return piece(scode, rcode.at[chaos], sc, qc, i)

    def x_copy(i):
        return piece(
            sbx.at[pl.ds(2 * i, 2), pl.ds(0, slots)], rx.at[chaos, :, pl.ds(0, slots)], sx, qx, i
        )

    def f_copy(i):
        return piece(
            sbf.at[pl.ds(2 * i, 2), pl.ds(0, slots)], rf.at[chaos, :, pl.ds(0, slots)], sf, qf, i
        )

    def keep_code(i):
        rcode[chaos] = scode[...]

    def keep(land, send):
        def run(i):
            for c in range(2):
                land[chaos, c, 0:slots, :] = send[2 * i + c, 0:slots, :]

        return run

    def packed(src, dst):
        def run(i):
            for c in range(2):
                dst[2 * i + c, 0:slots, :] = src[pl.ds(2 * i + c, slots, stride=cols), :]

        return run

    sibling = me + 1 - 2 * core
    coef_copy = remote(scoef.at[1], rcoef, sk, qk, device(sibling))
    scatter(code_copy, keep_code)
    coef_copy.start()
    scatter(x_copy, keep(rx, sbx), packed(x_ref, sbx))

    def code_wait(g):
        return remote(scode, rcode.at[g], sc.at[0], qc.at[g], device(me))

    def x_wait(g):
        return remote(
            sbx.at[0:2, pl.ds(0, slots)], rx.at[g, :, pl.ds(0, slots)], sx.at[0], qx.at[g], device(me)
        )

    def f_wait(g):
        return remote(
            sbf.at[0:2, pl.ds(0, slots)], rf.at[g, :, pl.ds(0, slots)], sf.at[0], qf.at[g], device(me)
        )

    arrive(code_wait)
    loads[4].wait()
    sub40 = lax.broadcasted_iota(jnp.int32, (PAD, LANES), 0)
    lane40 = lax.broadcasted_iota(jnp.int32, (PAD, LANES), 1)
    for g in range(8):
        spread = jnp.where(sub40 == lane40, rcode[g, 0:1, :], 0.0)
        placed = jnp.sum(spread, axis=1, keepdims=True)
        pick[PAD * g : PAD * (g + 1), :] = jnp.where(placed == code_ref[0:1, :], 1.0, 0.0)

    def parts(value):
        high = value.astype(jnp.bfloat16)
        rest = value - high.astype(F32)
        mid = rest.astype(jnp.bfloat16)
        low = (rest - mid.astype(F32)).astype(jnp.bfloat16)
        return [high, mid, low]

    def select(first, second, transposed):
        both = parts(first) + parts(second)
        return lax.dot_general(
            pick[...].astype(jnp.bfloat16),
            jnp.concatenate(both, axis=1),
            (((0 if transposed else 1,), (0,)), ((), ())),
            preferred_element_type=F32,
        )

    def column(result, c):
        base = 3 * LANES * c
        return (
            result[:, base : base + LANES]
            + result[:, base + LANES : base + 2 * LANES]
            + result[:, base + 2 * LANES : base + 3 * LANES]
        )

    loads[5].wait()
    sent(x_copy)
    scatter(f_copy, keep(rf, sbf), packed(f_ref, sbf))

    coef_copy.wait_recv()
    local = core == zz
    for c in range(2):
        field[0, c, rows:full, :] = jnp.where(local, scoef[0, c], rcoef[c])

    arrive(x_wait)
    got = select(rx[:, 0].reshape(8 * PAD, LANES), rx[:, 1].reshape(8 * PAD, LANES), True)
    for c in range(2):
        field[0, c, 0:rows, :] = column(got, c)[0:rows]

    def halo_left(i, count):
        return remote(
            field.at[i, 0, pl.ds(0, count)],
            halo.at[i, 1, pl.ds(0, count)],
            sh.at[i, 0],
            qh.at[i, 1],
            device(me - 1),
        )

    def halo_right(i, count):
        return remote(
            field.at[i, 1, pl.ds(0, count)],
            halo.at[i, 0, pl.ds(0, count)],
            sh.at[i, 1],
            qh.at[i, 0],
            device(me + 1),
        )

    def halo_start(i, count):
        pl.when(me > 0)(lambda: halo_left(i, count).start())
        pl.when(me < last)(lambda: halo_right(i, count).start())

    def halo_wait(i, count):
        pl.when(me > 0)(lambda: halo_right(i, count).wait_recv())
        pl.when(me < last)(lambda: halo_left(i, count).wait_recv())

    def halo_sent(i, count):
        pl.when(me > 0)(lambda: halo_left(i, count).wait_send())
        pl.when(me < last)(lambda: halo_right(i, count).wait_send())

    halo_start(0, full)

    lane8 = lax.broadcasted_iota(jnp.int32, (8, LANES), 1)

    def back_copy(i, g):
        return remote(
            outs.at[i, g, :, pl.ds(0, slots)],
            back.at[i, pl.ds(2 * (me % 8), 2), pl.ds(0, slots)],
            so.at[i, g],
            qo.at[i, me % 8],
            (me // 8, g),
        )

    def back_wait(i, j):
        return remote(
            outs.at[i, 0, :, pl.ds(0, slots)],
            back.at[i, pl.ds(2 * j, 2), pl.ds(0, slots)],
            so.at[i, 0],
            qo.at[i, j],
            (space, chaos),
        )

    def prepare_back(i):
        got = select(field[i + 1, 0, 0:rows, :], field[i + 1, 1, 0:rows, :], False)
        for c in range(2):
            whole = column(got, c)
            for g in range(8):
                outs[i, g, c] = whole[PAD * g : PAD * (g + 1)]

    def send_back(i):
        for o in range(8):
            g = (o + chaos) % 8
            here = jnp.logical_and(own_source, g == chaos)
            pl.when(jnp.logical_not(here))(lambda: back_copy(i, g).start())

            @pl.when(here)
            def _():
                back[i, pl.ds(2 * (me % 8), 2), 0:slots] = outs[i, g, :, 0:slots]

    def dots(which, values):
        dot_local[which] = zero8
        for n, value in enumerate(values):
            dot_local[which, n : n + 1, :] = jnp.sum(value, axis=0, keepdims=True)

    def dot_a_copy(which, o):
        return remote(
            dot_local.at[which],
            dot_a.at[which, member],
            sda.at[which, o],
            qda.at[which, member],
            device(16 * pair + (member + o) % 16),
        )

    def dot_b_copy(which, o):
        return remote(
            dot_b_local.at[which],
            dot_b.at[which, pair],
            sdb.at[which, o],
            qdb.at[which, pair],
            device(16 * ((pair + o) % 8) + member),
        )

    def dot_a_start(which):
        for o in range(1, 16):
            dot_a_copy(which, o).start()
        dot_a[which, member] = dot_local[which]

    def dot_b_start(which):
        for o in range(1, 16):
            m = (member + o) % 16
            remote(
                dot_local.at[which], dot_a.at[which, m], sda.at[which, 0], qda.at[which, m], device(me)
            ).wait_recv()
        total = dot_a[which, 0]
        for m in range(1, 16):
            total = total + dot_a[which, m]
        dot_b_local[which] = total
        for o in range(1, 8):
            dot_b_copy(which, o).start()
        dot_b[which, pair] = total

    def dot_total(which):
        for o in range(1, 8):
            m = (pair + o) % 8
            remote(
                dot_b_local.at[which], dot_b.at[which, m], sdb.at[which, 0], qdb.at[which, m], device(me)
            ).wait_recv()
        total = dot_b[which, 0]
        for m in range(1, 8):
            total = total + dot_b[which, m]
        return jnp.sum(total, axis=1, keepdims=True)

    halo_wait(0, full)
    for h in range(2):
        part = pl.ds(rows + 8 * h, 8)
        left, c0, c1, right = halo[0, 0, part], field[0, 0, part], field[0, 1, part], halo[0, 1, part]

        def up(value):
            return jnp.where(lane8 < LANES - 1, pltpu.roll(value, LANES - 1, 1), 0.0)

        kinds = [
            0.5 * (left + c0),
            0.5 * (c0 + c1),
            0.5 * (c1 + right),
            0.5 * (c0 + up(c0)),
            0.5 * (c1 + up(c1)),
            jnp.where(lane8 == 0, 0.5 * c0, 0.0),
            jnp.where(lane8 == 0, 0.5 * c1, 0.0),
            zero8,
        ]
        for n, kind in enumerate(kinds):
            faces[pl.ds(64 * h + n, 8, stride=8), :] = kind

    def total_of(sums):
        return [sums[n : n + 1] for n in range(3)]

    def gradients(i):
        for b in range(rows // 8):
            part = pl.ds(8 * b, 8)
            left, u0, u1, right = halo[i, 0, part], field[i, 0, part], field[i, 1, part], halo[i, 1, part]
            up0 = jnp.where(lane8 < LANES - 1, pltpu.roll(u0, LANES - 1, 1), 0.0)
            up1 = jnp.where(lane8 < LANES - 1, pltpu.roll(u1, LANES - 1, 1), 0.0)
            kinds = [u0 - left, u1 - u0, right - u1, up0 - u0, up1 - u1]
            kinds += [jnp.where(lane8 == 0, u0, 0.0), jnp.where(lane8 == 0, u1, 0.0), zero8]
            for n, kind in enumerate(kinds):
                grad[pl.ds(64 * b + n, 8, stride=8), :] = kind

    def mixing():
        weight = [faces[8 * k : 8 * (k + 1), :] for k in range(modes + 1)]
        for s, term in enumerate(terms):
            total = weight[0] * grad[8 * s : 8 * (s + 1), :]
            for k in range(modes):
                mix = None
                for step, square in ((1, term[k] + 1), (-1, term[k])):
                    near = term[:k] + (term[k] + step,) + term[k + 1 :]
                    if near not in position:
                        continue
                    at = position[near]
                    value = grad[8 * at : 8 * (at + 1), :]
                    if square > 1:
                        value = math.sqrt(square) * value
                    mix = value if mix is None else mix + value
                if mix is not None:
                    total = total + weight[k + 1] * mix
            flux[8 * s : 8 * (s + 1), :] = total
        for s in range(len(terms), rows):
            flux[8 * s : 8 * (s + 1), :] = zero8

    def divergence(i, after):
        for b in range(rows // 8):
            kind = [flux[pl.ds(64 * b + n, 8, stride=8), :] for n in range(7)]
            part = pl.ds(8 * b, 8)
            for c in range(2):
                down = jnp.where(lane8 > 0, pltpu.roll(kind[3 + c], 1, 1), kind[5 + c])
                after(c, part, kind[c] - kind[c + 1] + down - kind[3 + c])

    gradients(0)
    mixing()
    arrive(f_wait)
    got = select(rf[:, 0].reshape(8 * PAD, LANES), rf[:, 1].reshape(8 * PAD, LANES), True)
    for c in range(2):
        forced[c] = column(got, c)[0:rows]

    def first(c, part, value):
        field[1, c, part, :] = forced[c, part, :] - value

    divergence(0, first)
    halo_start(1, rows)
    prepare_back(0)
    halo_wait(1, rows)
    send_back(0)

    gradients(1)
    mixing()
    sums = [zero8, zero8]

    def second(c, part, value):
        field[2, c, part, :] = value
        r = field[1, c, part, :]
        sums[0] = sums[0] + r * r
        sums[1] = sums[1] + r * value

    divergence(1, second)
    halo_start(2, rows)
    dots(0, sums)
    dot_a_start(0)
    prepare_back(1)
    halo_wait(2, rows)
    dot_b_start(0)
    send_back(1)

    gradients(2)
    mixing()
    rr, rw = total_of(dot_total(0))[0:2]
    alpha = rr / rw
    sums = [zero8, zero8, zero8]

    def third(c, part, value):
        field[3, c, part, :] = value
        r, w = field[1, c, part, :], field[2, c, part, :]
        r1 = r - alpha * w
        ar1 = w - alpha * value
        sums[0] = sums[0] + r1 * r1
        sums[1] = sums[1] + r1 * ar1
        sums[2] = sums[2] + (r1 * w + r * ar1)

    divergence(2, third)
    dots(1, sums)
    dot_a_start(1)
    prepare_back(2)
    send_back(2)
    dot_b_start(1)
    rr1, rar, cross = total_of(dot_total(1))
    beta = rr1 / rr
    step = rr1 / (rar + beta * cross + beta * beta * rw)

    for j in range(8):
        here = jnp.logical_and(own_source, me % 8 == j)
        for i in range(3):
            pl.when(jnp.logical_not(here))(lambda: back_wait(i, j).wait_recv())

    for c in range(cols):
        r0, w, v = back[0, c, 0:slots], back[1, c, 0:slots], back[2, c, 0:slots]
        x = x_ref[pl.ds(c, slots, stride=cols), :]
        xo_ref[pl.ds(c, slots, stride=cols), :] = x + (alpha + step + step * beta) * r0 - (step * alpha) * w
        r1 = r0 - alpha * w
        ro_ref[pl.ds(c, slots, stride=cols), :] = r1 - step * (w - alpha * v + beta * w)

    sent(code_copy)
    sent(f_copy)
    coef_copy.wait_send()
    for i in range(3):
        halo_sent(i, rows if i else full)
        for g in range(8):
            here = jnp.logical_and(own_source, chaos == g)
            pl.when(jnp.logical_not(here))(lambda: back_copy(i, g).wait_send())
    for which in range(2):
        for o in range(1, 16):
            dot_a_copy(which, o).wait_send()
        for o in range(1, 8):
            dot_b_copy(which, o).wait_send()


def per_device(forcing, start_guess, mean_field, mode_fields, multi_index, coupled_slot):
    slots, cols, lanes = forcing.shape
    modes = mode_fields.shape[0]
    terms = term_list(modes, DEGREE)
    rows = -(-len(terms) // 8) * 8
    full = rows + 16
    wide = rows
    codes = np.full((8, wide), -2.0, np.float32)
    codes[:, : len(terms)] = [code_of(t) for t in terms]
    cfg = dict(slots=slots, cols=cols, terms=terms, modes=modes, rows=rows, full=full)
    flat = jax.ShapeDtypeStruct((slots * cols, lanes), F32)
    vmem = pl.BlockSpec(memory_space=pltpu.VMEM)
    hbm = pl.BlockSpec(memory_space=pltpu.HBM)
    dma, V = pltpu.SemaphoreType.DMA, pltpu.VMEM
    scratch = [
        V((slots * cols, lanes), F32),
        V((slots * cols, lanes), F32),
        V((cols, lanes), F32),
        V((modes, cols, lanes), F32),
        V((modes, slots), jnp.int32),
        V((8, wide), F32),
        dma((6,)),
        V((cols, PAD, lanes), F32),
        V((cols, PAD, lanes), F32),
        V((8, lanes), F32),
        V((2, 2, 16, lanes), F32),
        V((8, 2, PAD, lanes), F32),
        V((8, 2, PAD, lanes), F32),
        V((8, 8, lanes), F32),
        V((2, 16, lanes), F32),
        V((8 * PAD, wide), F32),
        V((4, 2, full, lanes), F32),
        V((2, rows, lanes), F32),
        V((3, 2, full, lanes), F32),
        V((8 * rows, lanes), F32),
        V((8 * rows, lanes), F32),
        V((128, lanes), F32),
        V((3, 8, 2, PAD, lanes), F32),
        V((3, cols, PAD, lanes), F32),
        V((2, 8, lanes), F32),
        V((2, 16, 8, lanes), F32),
        V((2, 8, lanes), F32),
        V((2, 8, 8, lanes), F32),
        dma((8,)),
        dma((8,)),
        dma((8,)),
        dma,
        dma((3, 2)),
        dma((3, 8)),
        dma((2, 16)),
        dma((2, 8)),
        dma((8,)),
        dma((8,)),
        dma((8,)),
        dma,
        dma((3, 2)),
        dma((3, 8)),
        dma((2, 16)),
        dma((2, 8)),
    ]
    x, r = pl.pallas_call(
        functools.partial(kernel, cfg),
        out_shape=(flat, flat),
        in_specs=[hbm] * 6,
        out_specs=(vmem, vmem),
        scratch_shapes=scratch,
        compiler_params=pltpu.CompilerParams(
            collective_id=0, has_side_effects=True, vmem_limit_bytes=64 * 2**20
        ),
    )(
        forcing.reshape(slots * cols, lanes),
        start_guess.reshape(slots * cols, lanes),
        mean_field,
        mode_fields,
        multi_index.T,
        jnp.asarray(codes),
    )
    return (x.reshape(slots, cols, lanes), r.reshape(slots, cols, lanes))


def solution(mesh):
    placed = (
        P("chaos", "space", None),
        P("chaos", "space", None),
        P("space", None),
        P(None, "space", None),
        P("chaos", None),
        P("chaos", None),
    )
    return jax.shard_map(
        per_device,
        mesh=mesh,
        in_specs=placed,
        out_specs=(P("chaos", "space", None), P("chaos", "space", None)),
        check_vma=False,
    )
```

```python
import functools
import math

import jax
import jax.numpy as jnp
import numpy as np
from jax import lax
from jax.experimental import pallas as pl
from jax.experimental.pallas import tpu as pltpu
from jax.sharding import PartitionSpec as P

MESH = pl.DeviceIdType.MESH
F32 = jnp.float32
DEGREE = 3
LANES = 128
PAD = 40
CUTS = 4


def term_list(modes, degree):
    def build(count, left):
        if count == 0:
            return [()]
        return [(a,) + tail for a in range(left + 1) for tail in build(count - 1, left - a)]

    return sorted(build(modes, degree), key=sum)


def code_of(term):
    return sum(m * 4**k for k, m in enumerate(term))


def kernel(
    cfg,
    f_hbm,
    x_hbm,
    mean_hbm,
    modes_hbm,
    index_hbm,
    code_hbm,
    xo_ref,
    ro_ref,
    f_ref,
    x_ref,
    mean_ref,
    modes_ref,
    index_ref,
    code_ref,
    si,
    sbx,
    sbf,
    scode,
    scoef,
    rx,
    rf,
    rcode,
    rcoef,
    pick,
    field,
    forced,
    halo,
    grad,
    flux,
    faces,
    outs,
    back,
    dot_local,
    dot_a,
    dot_b_local,
    dot_b,
    sx,
    sf,
    sc,
    sk,
    sh,
    so,
    sda,
    sdb,
    qx,
    qf,
    qc,
    qk,
    qh,
    qo,
    qda,
    qdb,
):
    slots, cols, terms, modes = cfg["slots"], cfg["cols"], cfg["terms"], cfg["modes"]
    rows = cfg["rows"]
    full = cfg["full"]
    position = {t: i for i, t in enumerate(terms)}

    space, chaos = lax.axis_index("space"), lax.axis_index("chaos")
    pair, core = space // 2, space % 2
    xx, zz = chaos // 2, chaos % 2
    lane_at = xx + zz * (3 - 2 * xx)
    member = 8 * zz + 2 * lane_at + core
    me = 16 * pair + member
    last = 127

    def device(j):
        p = (j // 2) % 8
        z = p // 4
        inner = p % 4
        x = inner + z * (3 - 2 * inner)
        return (2 * (j // 16) + j % 2, 2 * x + z)

    yy, high = pair // 2, pair % 2
    column_rank = 4 * high + 2 * zz + core
    plane_rank = 4 * yy + xx

    def in_column(r):
        return (4 * yy + 2 * (r // 4) + r % 2, 2 * xx + (r // 2) % 2)

    def in_plane(r):
        return (4 * (r // 4) + 2 * high + core, 2 * (r % 4) + zz)

    def remote(src, dst, ssem, rsem, where):
        return pltpu.make_async_remote_copy(
            src_ref=src, dst_ref=dst, send_sem=ssem, recv_sem=rsem, device_id=where, device_id_type=MESH
        )

    loads = [
        pltpu.make_async_copy(src, dst, si.at[n])
        for n, (src, dst) in enumerate(
            (
                (index_hbm, index_ref),
                (x_hbm, x_ref),
                (mean_hbm, mean_ref),
                (modes_hbm, modes_ref),
                (code_hbm, code_ref),
                (f_hbm, f_ref),
            )
        )
    ]
    for load in loads:
        load.start()

    zero8 = jnp.zeros((8, LANES), F32)
    for g in range(8):
        for c in range(2):
            rx[g, c, 32:40, :] = zero8
            rf[g, c, 32:40, :] = zero8

    @pl.when(me == 0)
    def _():
        for i in range(3):
            halo[i, 0] = jnp.zeros((full, LANES), F32)

    @pl.when(me == last)
    def _():
        for i in range(3):
            halo[i, 1] = jnp.zeros((full, LANES), F32)

    barrier = pltpu.get_barrier_semaphore()

    def greet(where):
        pl.semaphore_signal(barrier, inc=1, device_id=where, device_id_type=MESH)

    for o in range(1, 16):
        greet(in_plane((plane_rank + o) % 16))
    for o in range(1, 8):
        greet(in_column((column_rank + o) % 8))
    for dx in range(1, 4):
        for other_z, other_core in ((0, 1), (1, 0), (1, 1)):
            greet((2 * pair + (core + other_core) % 2, 2 * ((xx + dx) % 4) + (zz + other_z) % 2))
    pl.when(me > 0)(lambda: greet(device(me - 1)))
    pl.when(me < last)(lambda: greet(device(me + 1)))

    loads[0].wait()
    power = jnp.left_shift(1, 2 * lax.broadcasted_iota(jnp.int32, (modes, slots), 0)).astype(F32)
    code = jnp.sum(index_ref[...].astype(F32) * power, axis=0, keepdims=True)
    scode[...] = jnp.full((8, LANES), -1.0, F32)
    scode[:, 0:slots] = jnp.broadcast_to(code, (8, slots))

    loads[2].wait()
    loads[3].wait()
    mine = 2 * lane_at + core
    other = 2 * lane_at + (1 - core)
    for which, first in ((0, 2 * mine), (1, 2 * other)):
        for c in range(2):
            scoef[which, c, 8:16, :] = zero8
            scoef[which, c, 0:1, :] = mean_ref[pl.ds(first + c, 1), :]
            for k in range(modes):
                scoef[which, c, 1 + k : 2 + k, :] = modes_ref[k, pl.ds(first + c, 1), :]

    loads[1].wait()
    greeted = 15 + 7 + 9 + jnp.where(me > 0, 1, 0) + jnp.where(me < last, 1, 0)
    pl.semaphore_wait(barrier, greeted)

    def piece(send, land, ssem, rsem, i):
        where = device(8 * space + i)
        return remote(send, land, ssem.at[i], rsem.at[chaos], where)

    def far_first(o):
        target_x = (xx + (2, 2, 1, 1, 3, 3, 0, 0)[o]) % 4
        return 2 * (target_x + core * (3 - 2 * target_x)) + o % 2

    def scatter(copy_of, keep, ready=None):
        for o in range(8):
            i = far_first(o)
            target = 8 * space + i
            if ready is not None:
                ready(i)
            pl.when(target != me)(lambda: copy_of(i).start())
            pl.when(target == me)(lambda: keep(i))

    def sent(copy_of):
        for i in range(8):
            target = 8 * space + i
            pl.when(target != me)(lambda: copy_of(i).wait_send())

    own_source = (me // 8) == space

    def arrive(copy_of):
        for g in range(8):
            here = jnp.logical_and(own_source, chaos == g)
            pl.when(jnp.logical_not(here))(lambda: copy_of(g).wait_recv())

    def code_copy(i):
        return piece(scode, rcode.at[chaos], sc, qc, i)

    def x_copy(i):
        return piece(
            sbx.at[pl.ds(2 * i, 2), pl.ds(0, slots)], rx.at[chaos, :, pl.ds(0, slots)], sx, qx, i
        )

    def f_copy(i):
        return piece(
            sbf.at[pl.ds(2 * i, 2), pl.ds(0, slots)], rf.at[chaos, :, pl.ds(0, slots)], sf, qf, i
        )

    def keep_code(i):
        rcode[chaos] = scode[...]

    def keep(land, send):
        def run(i):
            for c in range(2):
                land[chaos, c, 0:slots, :] = send[2 * i + c, 0:slots, :]

        return run

    def packed(src, dst):
        def run(i):
            for c in range(2):
                dst[2 * i + c, 0:slots, :] = src[pl.ds(2 * i + c, slots, stride=cols), :]

        return run

    sibling = me + 1 - 2 * core
    coef_copy = remote(scoef.at[1], rcoef, sk, qk, device(sibling))
    scatter(code_copy, keep_code)
    coef_copy.start()
    scatter(x_copy, keep(rx, sbx), packed(x_ref, sbx))
    loads[5].wait()
    scatter(f_copy, keep(rf, sbf), packed(f_ref, sbf))

    def code_wait(g):
        return remote(scode, rcode.at[g], sc.at[0], qc.at[g], device(me))

    def x_wait(g):
        return remote(
            sbx.at[0:2, pl.ds(0, slots)], rx.at[g, :, pl.ds(0, slots)], sx.at[0], qx.at[g], device(me)
        )

    def f_wait(g):
        return remote(
            sbf.at[0:2, pl.ds(0, slots)], rf.at[g, :, pl.ds(0, slots)], sf.at[0], qf.at[g], device(me)
        )

    arrive(code_wait)
    loads[4].wait()
    sub40 = lax.broadcasted_iota(jnp.int32, (PAD, LANES), 0)
    lane40 = lax.broadcasted_iota(jnp.int32, (PAD, LANES), 1)
    for g in range(8):
        spread = jnp.where(sub40 == lane40, rcode[g, 0:1, :], 0.0)
        placed = jnp.sum(spread, axis=1, keepdims=True)
        pick[PAD * g : PAD * (g + 1), :] = jnp.where(placed == code_ref[0:1, :], 1.0, 0.0)

    def parts(value):
        high = value.astype(jnp.bfloat16)
        rest = value - high.astype(F32)
        mid = rest.astype(jnp.bfloat16)
        low = (rest - mid.astype(F32)).astype(jnp.bfloat16)
        return [high, mid, low]

    def select(first, second, transposed):
        both = parts(first) + parts(second)
        return lax.dot_general(
            pick[...].astype(jnp.bfloat16),
            jnp.concatenate(both, axis=1),
            (((0 if transposed else 1,), (0,)), ((), ())),
            preferred_element_type=F32,
        )

    def column(result, c):
        base = 3 * LANES * c
        return (
            result[:, base : base + LANES]
            + result[:, base + LANES : base + 2 * LANES]
            + result[:, base + 2 * LANES : base + 3 * LANES]
        )

    per = rows // CUTS

    def cut(k):
        return pl.ds(per * k, per) if k < CUTS else pl.ds(rows, full - rows)

    def halo_left(i, k):
        return remote(
            field.at[i, 0, cut(k)], halo.at[i, 1, cut(k)], sh.at[i, k, 0], qh.at[i, k, 1], device(me - 1)
        )

    def halo_right(i, k):
        return remote(
            field.at[i, 1, cut(k)], halo.at[i, 0, cut(k)], sh.at[i, k, 1], qh.at[i, k, 0], device(me + 1)
        )

    def halo_start(i, k):
        pl.when(me > 0)(lambda: halo_left(i, k).start())
        pl.when(me < last)(lambda: halo_right(i, k).start())

    def halo_wait(i, k):
        pl.when(me > 0)(lambda: halo_right(i, k).wait_recv())
        pl.when(me < last)(lambda: halo_left(i, k).wait_recv())

    def halo_sent(i, k):
        pl.when(me > 0)(lambda: halo_left(i, k).wait_send())
        pl.when(me < last)(lambda: halo_right(i, k).wait_send())

    coef_copy.wait_recv()
    local = core == zz
    for c in range(2):
        field[0, c, rows:full, :] = jnp.where(local, scoef[0, c], rcoef[c])
    halo_start(0, CUTS)

    arrive(x_wait)
    got = select(rx[:, 0].reshape(8 * PAD, LANES), rx[:, 1].reshape(8 * PAD, LANES), True)
    for c in range(2):
        field[0, c, 0:rows, :] = column(got, c)[0:rows]

    for k in range(CUTS):
        halo_start(0, k)

    lane8 = lax.broadcasted_iota(jnp.int32, (8, LANES), 1)

    def back_copy(i, g):
        return remote(
            outs.at[i, g, :, pl.ds(0, slots)],
            back.at[i, pl.ds(2 * (me % 8), 2), pl.ds(0, slots)],
            so.at[i, g],
            qo.at[i, me % 8],
            (me // 8, g),
        )

    def back_wait(i, j):
        return remote(
            outs.at[i, 0, :, pl.ds(0, slots)],
            back.at[i, pl.ds(2 * j, 2), pl.ds(0, slots)],
            so.at[i, 0],
            qo.at[i, j],
            (space, chaos),
        )

    def prepare_back(i):
        got = select(field[i + 1, 0, 0:rows, :], field[i + 1, 1, 0:rows, :], False)
        for c in range(2):
            whole = column(got, c)
            for g in range(8):
                outs[i, g, c] = whole[PAD * g : PAD * (g + 1)]

    def send_back(i):
        for o in range(8):
            g = (o + chaos) % 8
            here = jnp.logical_and(own_source, g == chaos)
            pl.when(jnp.logical_not(here))(lambda: back_copy(i, g).start())

            @pl.when(here)
            def _():
                back[i, pl.ds(2 * (me % 8), 2), 0:slots] = outs[i, g, :, 0:slots]

    def dots(which, values):
        dot_local[which] = zero8
        for n, value in enumerate(values):
            dot_local[which, n : n + 1, :] = jnp.sum(value, axis=0, keepdims=True)

    def dot_a_copy(which, o):
        return remote(
            dot_local.at[which],
            dot_a.at[which, column_rank],
            sda.at[which, o],
            qda.at[which, column_rank],
            in_column((column_rank + o) % 8),
        )

    def dot_b_copy(which, o):
        return remote(
            dot_b_local.at[which],
            dot_b.at[which, plane_rank],
            sdb.at[which, o],
            qdb.at[which, plane_rank],
            in_plane((plane_rank + o) % 16),
        )

    def dot_a_start(which):
        for o in range(1, 8):
            dot_a_copy(which, o).start()
        dot_a[which, column_rank] = dot_local[which]

    def dot_b_start(which):
        for o in range(1, 8):
            m = (column_rank + o) % 8
            remote(
                dot_local.at[which], dot_a.at[which, m], sda.at[which, 0], qda.at[which, m], device(me)
            ).wait_recv()
        total = dot_a[which, 0]
        for m in range(1, 8):
            total = total + dot_a[which, m]
        dot_b_local[which] = total
        for o in range(1, 16):
            dot_b_copy(which, o).start()
        dot_b[which, plane_rank] = total

    def dot_total(which):
        for o in range(1, 16):
            m = (plane_rank + o) % 16
            remote(
                dot_b_local.at[which], dot_b.at[which, m], sdb.at[which, 0], qdb.at[which, m], device(me)
            ).wait_recv()
        total = dot_b[which, 0]
        for m in range(1, 16):
            total = total + dot_b[which, m]
        return jnp.sum(total, axis=1, keepdims=True)

    halo_wait(0, CUTS)
    for h in range(2):
        part = pl.ds(rows + 8 * h, 8)
        left, c0, c1, right = halo[0, 0, part], field[0, 0, part], field[0, 1, part], halo[0, 1, part]

        def up(value):
            return jnp.where(lane8 < LANES - 1, pltpu.roll(value, LANES - 1, 1), 0.0)

        kinds = [
            0.5 * (left + c0),
            0.5 * (c0 + c1),
            0.5 * (c1 + right),
            0.5 * (c0 + up(c0)),
            0.5 * (c1 + up(c1)),
            jnp.where(lane8 == 0, 0.5 * c0, 0.0),
            jnp.where(lane8 == 0, 0.5 * c1, 0.0),
            zero8,
        ]
        for n, kind in enumerate(kinds):
            faces[pl.ds(64 * h + n, 8, stride=8), :] = kind

    def total_of(sums):
        return [sums[n : n + 1] for n in range(3)]

    def gradients(i):
        for b in range(rows // 8):
            if 8 * b % per == 0:
                halo_wait(i, 8 * b // per)
            part = pl.ds(8 * b, 8)
            left, u0, u1, right = halo[i, 0, part], field[i, 0, part], field[i, 1, part], halo[i, 1, part]
            up0 = jnp.where(lane8 < LANES - 1, pltpu.roll(u0, LANES - 1, 1), 0.0)
            up1 = jnp.where(lane8 < LANES - 1, pltpu.roll(u1, LANES - 1, 1), 0.0)
            kinds = [u0 - left, u1 - u0, right - u1, up0 - u0, up1 - u1]
            kinds += [jnp.where(lane8 == 0, u0, 0.0), jnp.where(lane8 == 0, u1, 0.0), zero8]
            for n, kind in enumerate(kinds):
                grad[pl.ds(64 * b + n, 8, stride=8), :] = kind

    def mixing():
        weight = [faces[8 * k : 8 * (k + 1), :] for k in range(modes + 1)]
        for s, term in enumerate(terms):
            total = weight[0] * grad[8 * s : 8 * (s + 1), :]
            for k in range(modes):
                mix = None
                for step, square in ((1, term[k] + 1), (-1, term[k])):
                    near = term[:k] + (term[k] + step,) + term[k + 1 :]
                    if near not in position:
                        continue
                    at = position[near]
                    value = grad[8 * at : 8 * (at + 1), :]
                    if square > 1:
                        value = math.sqrt(square) * value
                    mix = value if mix is None else mix + value
                if mix is not None:
                    total = total + weight[k + 1] * mix
            flux[8 * s : 8 * (s + 1), :] = total
        for s in range(len(terms), rows):
            flux[8 * s : 8 * (s + 1), :] = zero8

    def divergence(i, after):
        for b in range(rows // 8):
            kind = [flux[pl.ds(64 * b + n, 8, stride=8), :] for n in range(7)]
            part = pl.ds(8 * b, 8)
            for c in range(2):
                down = jnp.where(lane8 > 0, pltpu.roll(kind[3 + c], 1, 1), kind[5 + c])
                after(c, part, kind[c] - kind[c + 1] + down - kind[3 + c])
            if i < 2 and 8 * (b + 1) % per == 0:
                halo_start(i + 1, 8 * b // per)

    gradients(0)
    mixing()
    arrive(f_wait)
    got = select(rf[:, 0].reshape(8 * PAD, LANES), rf[:, 1].reshape(8 * PAD, LANES), True)
    for c in range(2):
        forced[c] = column(got, c)[0:rows]

    def first(c, part, value):
        field[1, c, part, :] = forced[c, part, :] - value

    divergence(0, first)
    prepare_back(0)

    gradients(1)
    send_back(0)
    mixing()
    sums = [zero8, zero8]

    def second(c, part, value):
        field[2, c, part, :] = value
        r = field[1, c, part, :]
        sums[0] = sums[0] + r * r
        sums[1] = sums[1] + r * value

    divergence(1, second)
    dots(0, sums)
    dot_a_start(0)
    prepare_back(1)
    dot_b_start(0)

    gradients(2)
    send_back(1)
    mixing()
    rr, rw = total_of(dot_total(0))[0:2]
    alpha = rr / rw
    sums = [zero8, zero8, zero8]

    def third(c, part, value):
        field[3, c, part, :] = value
        r, w = field[1, c, part, :], field[2, c, part, :]
        r1 = r - alpha * w
        ar1 = w - alpha * value
        sums[0] = sums[0] + r1 * r1
        sums[1] = sums[1] + r1 * ar1
        sums[2] = sums[2] + (r1 * w + r * ar1)

    divergence(2, third)
    dots(1, sums)
    dot_a_start(1)
    prepare_back(2)
    send_back(2)
    dot_b_start(1)
    rr1, rar, cross = total_of(dot_total(1))
    beta = rr1 / rr
    step = rr1 / (rar + beta * cross + beta * beta * rw)

    for j in range(8):
        here = jnp.logical_and(own_source, me % 8 == j)
        for i in range(3):
            pl.when(jnp.logical_not(here))(lambda: back_wait(i, j).wait_recv())

    for c in range(cols):
        r0, w, v = back[0, c, 0:slots], back[1, c, 0:slots], back[2, c, 0:slots]
        x = x_ref[pl.ds(c, slots, stride=cols), :]
        xo_ref[pl.ds(c, slots, stride=cols), :] = x + (alpha + step + step * beta) * r0 - (step * alpha) * w
        r1 = r0 - alpha * w
        ro_ref[pl.ds(c, slots, stride=cols), :] = r1 - step * (w - alpha * v + beta * w)

    sent(code_copy)
    sent(x_copy)
    sent(f_copy)
    coef_copy.wait_send()
    for i in range(3):
        for k in range(CUTS if i else CUTS + 1):
            halo_sent(i, k)
        for g in range(8):
            here = jnp.logical_and(own_source, chaos == g)
            pl.when(jnp.logical_not(here))(lambda: back_copy(i, g).wait_send())
    for which in range(2):
        for o in range(1, 8):
            dot_a_copy(which, o).wait_send()
        for o in range(1, 16):
            dot_b_copy(which, o).wait_send()


def per_device(forcing, start_guess, mean_field, mode_fields, multi_index, coupled_slot):
    slots, cols, lanes = forcing.shape
    modes = mode_fields.shape[0]
    terms = term_list(modes, DEGREE)
    rows = -(-len(terms) // 8) * 8
    full = rows + 16
    wide = rows
    codes = np.full((8, wide), -2.0, np.float32)
    codes[:, : len(terms)] = [code_of(t) for t in terms]
    cfg = dict(slots=slots, cols=cols, terms=terms, modes=modes, rows=rows, full=full)
    flat = pltpu.VMEM((slots * cols, lanes), F32)
    vmem = pl.BlockSpec(memory_space=pltpu.VMEM)
    hbm = pl.BlockSpec(memory_space=pltpu.HBM)
    dma, V = pltpu.SemaphoreType.DMA, pltpu.VMEM
    scratch = [
        V((slots * cols, lanes), F32),
        V((slots * cols, lanes), F32),
        V((cols, lanes), F32),
        V((modes, cols, lanes), F32),
        V((modes, slots), jnp.int32),
        V((8, wide), F32),
        dma((6,)),
        V((cols, PAD, lanes), F32),
        V((cols, PAD, lanes), F32),
        V((8, lanes), F32),
        V((2, 2, 16, lanes), F32),
        V((8, 2, PAD, lanes), F32),
        V((8, 2, PAD, lanes), F32),
        V((8, 8, lanes), F32),
        V((2, 16, lanes), F32),
        V((8 * PAD, wide), F32),
        V((4, 2, full, lanes), F32),
        V((2, rows, lanes), F32),
        V((3, 2, full, lanes), F32),
        V((8 * rows, lanes), F32),
        V((8 * rows, lanes), F32),
        V((128, lanes), F32),
        V((3, 8, 2, PAD, lanes), F32),
        V((3, cols, PAD, lanes), F32),
        V((2, 8, lanes), F32),
        V((2, 8, 8, lanes), F32),
        V((2, 8, lanes), F32),
        V((2, 16, 8, lanes), F32),
        dma((8,)),
        dma((8,)),
        dma((8,)),
        dma,
        dma((3, CUTS + 1, 2)),
        dma((3, 8)),
        dma((2, 8)),
        dma((2, 16)),
        dma((8,)),
        dma((8,)),
        dma((8,)),
        dma,
        dma((3, CUTS + 1, 2)),
        dma((3, 8)),
        dma((2, 8)),
        dma((2, 16)),
    ]
    x, r = pl.pallas_call(
        functools.partial(kernel, cfg),
        out_shape=(flat, flat),
        in_specs=[hbm] * 6,
        out_specs=(vmem, vmem),
        scratch_shapes=scratch,
        compiler_params=pltpu.CompilerParams(
            collective_id=0, has_side_effects=True, vmem_limit_bytes=60 * 2**20
        ),
    )(
        forcing.reshape(slots * cols, lanes),
        start_guess.reshape(slots * cols, lanes),
        mean_field,
        mode_fields,
        multi_index.T,
        jnp.asarray(codes),
    )
    return (x.reshape(slots, cols, lanes), r.reshape(slots, cols, lanes))


def solution(mesh):
    placed = (
        P("chaos", "space", None),
        P("chaos", "space", None),
        P("space", None),
        P(None, "space", None),
        P("chaos", None),
        P("chaos", None),
    )
    return jax.shard_map(
        per_device,
        mesh=mesh,
        in_specs=placed,
        out_specs=(P("chaos", "space", None), P("chaos", "space", None)),
        check_vma=False,
    )
```

```python
import functools
import math

import jax
import jax.numpy as jnp
import numpy as np
from jax import lax
from jax.experimental import pallas as pl
from jax.experimental.pallas import tpu as pltpu
from jax.sharding import PartitionSpec as P

MESH = pl.DeviceIdType.MESH
F32 = jnp.float32
DEGREE = 3
LANES = 128
PAD = 40


def term_list(modes, degree):
    def build(count, left):
        if count == 0:
            return [()]
        return [(a,) + tail for a in range(left + 1) for tail in build(count - 1, left - a)]

    return sorted(build(modes, degree), key=sum)


def code_of(term):
    return sum(m * 4**k for k, m in enumerate(term))


def kernel(
    cfg,
    f_hbm,
    x_hbm,
    mean_hbm,
    modes_hbm,
    index_hbm,
    code_hbm,
    xo_ref,
    ro_ref,
    f_ref,
    x_ref,
    mean_ref,
    modes_ref,
    index_ref,
    code_ref,
    si,
    sbx,
    sbf,
    scode,
    scoef,
    rx,
    rf,
    rcode,
    rcoef,
    pick,
    field,
    forced,
    halo,
    grad,
    flux,
    faces,
    outs,
    back,
    dot_local,
    dot_a,
    dot_b_local,
    dot_b,
    sx,
    sf,
    sc,
    sk,
    sh,
    so,
    sda,
    sdb,
    qx,
    qf,
    qc,
    qk,
    qh,
    qo,
    qda,
    qdb,
):
    slots, cols, terms, modes = cfg["slots"], cfg["cols"], cfg["terms"], cfg["modes"]
    rows = cfg["rows"]
    full = cfg["full"]
    position = {t: i for i, t in enumerate(terms)}

    space, chaos = lax.axis_index("space"), lax.axis_index("chaos")
    pair, core = space // 2, space % 2
    xx, zz = chaos // 2, chaos % 2
    lane_at = xx + zz * (3 - 2 * xx)
    member = 8 * zz + 2 * lane_at + core
    me = 16 * pair + member
    last = 127

    def device(j):
        p = (j // 2) % 8
        z = p // 4
        inner = p % 4
        x = inner + z * (3 - 2 * inner)
        return (2 * (j // 16) + j % 2, 2 * x + z)

    yy, high = pair // 2, pair % 2
    column_rank = 4 * high + 2 * zz + core
    plane_rank = 4 * yy + xx

    def in_column(r):
        return (4 * yy + 2 * (r // 4) + r % 2, 2 * xx + (r // 2) % 2)

    def in_plane(r):
        return (4 * (r // 4) + 2 * high + core, 2 * (r % 4) + zz)

    def remote(src, dst, ssem, rsem, where):
        return pltpu.make_async_remote_copy(
            src_ref=src, dst_ref=dst, send_sem=ssem, recv_sem=rsem, device_id=where, device_id_type=MESH
        )

    loads = [
        pltpu.make_async_copy(src, dst, si.at[n])
        for n, (src, dst) in enumerate(
            (
                (index_hbm, index_ref),
                (x_hbm, x_ref),
                (mean_hbm, mean_ref),
                (modes_hbm, modes_ref),
                (code_hbm, code_ref),
                (f_hbm, f_ref),
            )
        )
    ]
    for load in loads:
        load.start()

    zero8 = jnp.zeros((8, LANES), F32)
    for g in range(8):
        for c in range(2):
            rx[g, c, 32:40, :] = zero8
            rf[g, c, 32:40, :] = zero8

    @pl.when(me == 0)
    def _():
        for i in range(3):
            halo[i, 0] = jnp.zeros((full, LANES), F32)

    @pl.when(me == last)
    def _():
        for i in range(3):
            halo[i, 1] = jnp.zeros((full, LANES), F32)

    barrier = pltpu.get_barrier_semaphore()

    def greet(where):
        pl.semaphore_signal(barrier, inc=1, device_id=where, device_id_type=MESH)

    for o in range(1, 16):
        greet(in_plane((plane_rank + o) % 16))
    for o in range(1, 8):
        greet(in_column((column_rank + o) % 8))
    for dx in range(1, 4):
        for other_z, other_core in ((0, 1), (1, 0), (1, 1)):
            greet((2 * pair + (core + other_core) % 2, 2 * ((xx + dx) % 4) + (zz + other_z) % 2))
    pl.when(me > 0)(lambda: greet(device(me - 1)))
    pl.when(me < last)(lambda: greet(device(me + 1)))

    loads[0].wait()
    power = jnp.left_shift(1, 2 * lax.broadcasted_iota(jnp.int32, (modes, slots), 0)).astype(F32)
    code = jnp.sum(index_ref[...].astype(F32) * power, axis=0, keepdims=True)
    scode[...] = jnp.full((8, LANES), -1.0, F32)
    scode[:, 0:slots] = jnp.broadcast_to(code, (8, slots))

    loads[2].wait()
    loads[3].wait()
    mine = 2 * lane_at + core
    other = 2 * lane_at + (1 - core)
    for which, first in ((0, 2 * mine), (1, 2 * other)):
        for c in range(2):
            scoef[which, c, 8:16, :] = zero8
            scoef[which, c, 0:1, :] = mean_ref[pl.ds(first + c, 1), :]
            for k in range(modes):
                scoef[which, c, 1 + k : 2 + k, :] = modes_ref[k, pl.ds(first + c, 1), :]

    loads[1].wait()
    greeted = 15 + 7 + 9 + jnp.where(me > 0, 1, 0) + jnp.where(me < last, 1, 0)
    pl.semaphore_wait(barrier, greeted)

    def piece(send, land, ssem, rsem, i):
        where = device(8 * space + i)
        return remote(send, land, ssem, rsem, where)

    def far_first(o):
        target_x = (xx + (2, 2, 1, 1, 3, 3, 0, 0)[o]) % 4
        return 2 * (target_x + core * (3 - 2 * target_x)) + o % 2

    def scatter(copy_of, keep, ready=None):
        for o in range(8):
            i = far_first(o)
            target = 8 * space + i
            if ready is not None:
                ready(i)
            pl.when(target != me)(lambda: copy_of(i).start())
            pl.when(target == me)(lambda: keep(i))

    own_source = (me // 8) == space

    def whole(view, ssem, rsem):
        return remote(view, view, ssem, rsem, device(me))

    def arrive(view_of, ssem, rsem):
        pl.when(own_source)(lambda: whole(view_of(7), ssem, rsem).wait_recv())
        pl.when(jnp.logical_not(own_source))(lambda: whole(view_of(8), ssem, rsem).wait_recv())

    def sent(view_of, ssem, rsem):
        pl.when(own_source)(lambda: whole(view_of(7), ssem, rsem).wait_send())
        pl.when(jnp.logical_not(own_source))(lambda: whole(view_of(8), ssem, rsem).wait_send())

    def codes_of(n):
        return rcode.at[pl.ds(0, n)]

    def x_of(n):
        return rx.at[pl.ds(0, n), :, pl.ds(0, slots)]

    def f_of(n):
        return rf.at[pl.ds(0, n), :, pl.ds(0, slots)]

    def back_of(n):
        return back.at[:, pl.ds(0, 2 * n), pl.ds(0, slots)]

    def code_copy(i):
        return piece(scode, rcode.at[chaos], sc, qc, i)

    def x_copy(i):
        return piece(
            sbx.at[pl.ds(2 * i, 2), pl.ds(0, slots)], rx.at[chaos, :, pl.ds(0, slots)], sx, qx, i
        )

    def f_copy(i):
        return piece(
            sbf.at[pl.ds(2 * i, 2), pl.ds(0, slots)], rf.at[chaos, :, pl.ds(0, slots)], sf, qf, i
        )

    def keep_code(i):
        rcode[chaos] = scode[...]

    def keep(land, send):
        def run(i):
            for c in range(2):
                land[chaos, c, 0:slots, :] = send[2 * i + c, 0:slots, :]

        return run

    def packed(src, dst):
        def run(i):
            for c in range(2):
                dst[2 * i + c, 0:slots, :] = src[pl.ds(2 * i + c, slots, stride=cols), :]

        return run

    sibling = me + 1 - 2 * core
    coef_copy = remote(scoef.at[1], rcoef, sk, qk, device(sibling))
    scatter(code_copy, keep_code)
    coef_copy.start()
    scatter(x_copy, keep(rx, sbx), packed(x_ref, sbx))
    loads[5].wait()
    scatter(f_copy, keep(rf, sbf), packed(f_ref, sbf))

    arrive(codes_of, sc, qc)
    loads[4].wait()
    sub40 = lax.broadcasted_iota(jnp.int32, (PAD, LANES), 0)
    lane40 = lax.broadcasted_iota(jnp.int32, (PAD, LANES), 1)
    for g in range(8):
        spread = jnp.where(sub40 == lane40, rcode[g, 0:1, :], 0.0)
        placed = jnp.sum(spread, axis=1, keepdims=True)
        pick[PAD * g : PAD * (g + 1), :] = jnp.where(placed == code_ref[0:1, :], 1.0, 0.0)

    def parts(value):
        high = value.astype(jnp.bfloat16)
        rest = value - high.astype(F32)
        mid = rest.astype(jnp.bfloat16)
        low = (rest - mid.astype(F32)).astype(jnp.bfloat16)
        return [high, mid, low]

    def select(first, second, transposed):
        both = parts(first) + parts(second)
        return lax.dot_general(
            pick[...].astype(jnp.bfloat16),
            jnp.concatenate(both, axis=1),
            (((0 if transposed else 1,), (0,)), ((), ())),
            preferred_element_type=F32,
        )

    def column(result, c):
        base = 3 * LANES * c
        return (
            result[:, base : base + LANES]
            + result[:, base + LANES : base + 2 * LANES]
            + result[:, base + 2 * LANES : base + 3 * LANES]
        )

    def span(i):
        return pl.ds(0, rows if i else full)

    def halo_left(i):
        return remote(
            field.at[i, 0, span(i)], halo.at[i, 1, span(i)], sh.at[i, 0], qh.at[i, 1], device(me - 1)
        )

    def halo_right(i):
        return remote(
            field.at[i, 1, span(i)], halo.at[i, 0, span(i)], sh.at[i, 1], qh.at[i, 0], device(me + 1)
        )

    def halo_start(i):
        pl.when(me > 0)(lambda: halo_left(i).start())
        pl.when(me < last)(lambda: halo_right(i).start())

    def halo_wait(i):
        pl.when(me > 0)(lambda: halo_right(i).wait_recv())
        pl.when(me < last)(lambda: halo_left(i).wait_recv())

    def halo_sent(i):
        pl.when(me > 0)(lambda: halo_left(i).wait_send())
        pl.when(me < last)(lambda: halo_right(i).wait_send())

    coef_copy.wait_recv()
    local = core == zz
    for c in range(2):
        field[0, c, rows:full, :] = jnp.where(local, scoef[0, c], rcoef[c])

    arrive(x_of, sx, qx)
    got = select(rx[:, 0].reshape(8 * PAD, LANES), rx[:, 1].reshape(8 * PAD, LANES), True)
    for c in range(2):
        field[0, c, 0:rows, :] = column(got, c)[0:rows]

    halo_start(0)

    lane8 = lax.broadcasted_iota(jnp.int32, (8, LANES), 1)

    def back_copy(i, g):
        return remote(
            outs.at[i, g, :, pl.ds(0, slots)],
            back.at[i, pl.ds(2 * (me % 8), 2), pl.ds(0, slots)],
            so,
            qo,
            (me // 8, g),
        )

    def prepare_back(i):
        got = select(field[i + 1, 0, 0:rows, :], field[i + 1, 1, 0:rows, :], False)
        for c in range(2):
            whole = column(got, c)
            for g in range(8):
                outs[i, g, c] = whole[PAD * g : PAD * (g + 1)]

    def send_back(i):
        for o in range(8):
            g = (o + chaos) % 8
            here = jnp.logical_and(own_source, g == chaos)
            pl.when(jnp.logical_not(here))(lambda: back_copy(i, g).start())

            @pl.when(here)
            def _():
                back[i, pl.ds(2 * (me % 8), 2), 0:slots] = outs[i, g, :, 0:slots]

    def dots(which, values):
        dot_local[which] = zero8
        for n, value in enumerate(values):
            dot_local[which, n : n + 1, :] = jnp.sum(value, axis=0, keepdims=True)

    def dot_a_copy(which, o):
        return remote(
            dot_local.at[which],
            dot_a.at[which, column_rank],
            sda,
            qda.at[which],
            in_column((column_rank + o) % 8),
        )

    def dot_b_copy(which, o):
        return remote(
            dot_b_local.at[which],
            dot_b.at[which, plane_rank],
            sdb,
            qdb.at[which],
            in_plane((plane_rank + o) % 16),
        )

    def dot_a_start(which):
        for o in range(1, 8):
            dot_a_copy(which, o).start()
        dot_a[which, column_rank] = dot_local[which]

    def dot_b_start(which):
        whole(dot_a.at[which, pl.ds(0, 7)], sda, qda.at[which]).wait_recv()
        total = dot_a[which, 0]
        for m in range(1, 8):
            total = total + dot_a[which, m]
        dot_b_local[which] = total
        for o in range(1, 16):
            dot_b_copy(which, o).start()
        dot_b[which, plane_rank] = total

    def dot_total(which):
        whole(dot_b.at[which, pl.ds(0, 15)], sdb, qdb.at[which]).wait_recv()
        total = dot_b[which, 0]
        for m in range(1, 16):
            total = total + dot_b[which, m]
        return jnp.sum(total, axis=1, keepdims=True)

    halo_wait(0)
    for h in range(2):
        part = pl.ds(rows + 8 * h, 8)
        left, c0, c1, right = halo[0, 0, part], field[0, 0, part], field[0, 1, part], halo[0, 1, part]

        def up(value):
            return jnp.where(lane8 < LANES - 1, pltpu.roll(value, LANES - 1, 1), 0.0)

        kinds = [
            0.5 * (left + c0),
            0.5 * (c0 + c1),
            0.5 * (c1 + right),
            0.5 * (c0 + up(c0)),
            0.5 * (c1 + up(c1)),
            jnp.where(lane8 == 0, 0.5 * c0, 0.0),
            jnp.where(lane8 == 0, 0.5 * c1, 0.0),
            zero8,
        ]
        for n, kind in enumerate(kinds):
            faces[pl.ds(64 * h + n, 8, stride=8), :] = kind

    def total_of(sums):
        return [sums[n : n + 1] for n in range(3)]

    def gradients(i):
        if i:
            halo_wait(i)
        for b in range(rows // 8):
            part = pl.ds(8 * b, 8)
            left, u0, u1, right = halo[i, 0, part], field[i, 0, part], field[i, 1, part], halo[i, 1, part]
            up0 = jnp.where(lane8 < LANES - 1, pltpu.roll(u0, LANES - 1, 1), 0.0)
            up1 = jnp.where(lane8 < LANES - 1, pltpu.roll(u1, LANES - 1, 1), 0.0)
            kinds = [u0 - left, u1 - u0, right - u1, up0 - u0, up1 - u1]
            kinds += [jnp.where(lane8 == 0, u0, 0.0), jnp.where(lane8 == 0, u1, 0.0), zero8]
            for n, kind in enumerate(kinds):
                grad[pl.ds(64 * b + n, 8, stride=8), :] = kind

    def mixing():
        weight = [faces[8 * k : 8 * (k + 1), :] for k in range(modes + 1)]
        for s, term in enumerate(terms):
            total = weight[0] * grad[8 * s : 8 * (s + 1), :]
            for k in range(modes):
                mix = None
                for step, square in ((1, term[k] + 1), (-1, term[k])):
                    near = term[:k] + (term[k] + step,) + term[k + 1 :]
                    if near not in position:
                        continue
                    at = position[near]
                    value = grad[8 * at : 8 * (at + 1), :]
                    if square > 1:
                        value = math.sqrt(square) * value
                    mix = value if mix is None else mix + value
                if mix is not None:
                    total = total + weight[k + 1] * mix
            flux[8 * s : 8 * (s + 1), :] = total
        for s in range(len(terms), rows):
            flux[8 * s : 8 * (s + 1), :] = zero8

    def divergence(i, after):
        for b in range(rows // 8):
            kind = [flux[pl.ds(64 * b + n, 8, stride=8), :] for n in range(7)]
            part = pl.ds(8 * b, 8)
            for c in range(2):
                down = jnp.where(lane8 > 0, pltpu.roll(kind[3 + c], 1, 1), kind[5 + c])
                after(c, part, kind[c] - kind[c + 1] + down - kind[3 + c])

    gradients(0)
    mixing()
    arrive(f_of, sf, qf)
    got = select(rf[:, 0].reshape(8 * PAD, LANES), rf[:, 1].reshape(8 * PAD, LANES), True)
    for c in range(2):
        forced[c] = column(got, c)[0:rows]

    def first(c, part, value):
        field[1, c, part, :] = forced[c, part, :] - value

    divergence(0, first)
    halo_start(1)
    prepare_back(0)

    gradients(1)
    send_back(0)
    mixing()
    sums = [zero8, zero8]

    def second(c, part, value):
        field[2, c, part, :] = value
        r = field[1, c, part, :]
        sums[0] = sums[0] + r * r
        sums[1] = sums[1] + r * value

    divergence(1, second)
    halo_start(2)
    dots(0, sums)
    dot_a_start(0)
    prepare_back(1)
    dot_b_start(0)

    gradients(2)
    send_back(1)
    mixing()
    rr, rw = total_of(dot_total(0))[0:2]
    alpha = rr / rw
    sums = [zero8, zero8, zero8]

    def third(c, part, value):
        field[3, c, part, :] = value
        r, w = field[1, c, part, :], field[2, c, part, :]
        r1 = r - alpha * w
        ar1 = w - alpha * value
        sums[0] = sums[0] + r1 * r1
        sums[1] = sums[1] + r1 * ar1
        sums[2] = sums[2] + (r1 * w + r * ar1)

    divergence(2, third)
    dots(1, sums)
    dot_a_start(1)
    prepare_back(2)
    send_back(2)
    dot_b_start(1)
    rr1, rar, cross = total_of(dot_total(1))
    beta = rr1 / rr
    step = rr1 / (rar + beta * cross + beta * beta * rw)

    arrive(back_of, so, qo)

    for c in range(cols):
        r0, w, v = back[0, c, 0:slots], back[1, c, 0:slots], back[2, c, 0:slots]
        x = x_ref[pl.ds(c, slots, stride=cols), :]
        xo_ref[pl.ds(c, slots, stride=cols), :] = x + (alpha + step + step * beta) * r0 - (step * alpha) * w
        r1 = r0 - alpha * w
        ro_ref[pl.ds(c, slots, stride=cols), :] = r1 - step * (w - alpha * v + beta * w)

    sent(codes_of, sc, qc)
    sent(x_of, sx, qx)
    sent(f_of, sf, qf)
    sent(back_of, so, qo)
    coef_copy.wait_send()
    for i in range(3):
        halo_sent(i)
    whole(dot_a.at[:, pl.ds(0, 7)], sda, qda.at[0]).wait_send()
    whole(dot_b.at[:, pl.ds(0, 15)], sdb, qdb.at[0]).wait_send()


def per_device(forcing, start_guess, mean_field, mode_fields, multi_index, coupled_slot):
    slots, cols, lanes = forcing.shape
    modes = mode_fields.shape[0]
    terms = term_list(modes, DEGREE)
    rows = -(-len(terms) // 8) * 8
    full = rows + 16
    wide = rows
    codes = np.full((8, wide), -2.0, np.float32)
    codes[:, : len(terms)] = [code_of(t) for t in terms]
    cfg = dict(slots=slots, cols=cols, terms=terms, modes=modes, rows=rows, full=full)
    flat = pltpu.VMEM((slots * cols, lanes), F32)
    vmem = pl.BlockSpec(memory_space=pltpu.VMEM)
    hbm = pl.BlockSpec(memory_space=pltpu.HBM)
    dma, V = pltpu.SemaphoreType.DMA, pltpu.VMEM
    scratch = [
        V((slots * cols, lanes), F32),
        V((slots * cols, lanes), F32),
        V((cols, lanes), F32),
        V((modes, cols, lanes), F32),
        V((modes, slots), jnp.int32),
        V((8, wide), F32),
        dma((6,)),
        V((cols, PAD, lanes), F32),
        V((cols, PAD, lanes), F32),
        V((8, lanes), F32),
        V((2, 2, 16, lanes), F32),
        V((8, 2, PAD, lanes), F32),
        V((8, 2, PAD, lanes), F32),
        V((8, 8, lanes), F32),
        V((2, 16, lanes), F32),
        V((8 * PAD, wide), F32),
        V((4, 2, full, lanes), F32),
        V((2, rows, lanes), F32),
        V((3, 2, full, lanes), F32),
        V((8 * rows, lanes), F32),
        V((8 * rows, lanes), F32),
        V((128, lanes), F32),
        V((3, 8, 2, PAD, lanes), F32),
        V((3, cols, PAD, lanes), F32),
        V((2, 8, lanes), F32),
        V((2, 8, 8, lanes), F32),
        V((2, 8, lanes), F32),
        V((2, 16, 8, lanes), F32),
        dma,
        dma,
        dma,
        dma,
        dma((3, 2)),
        dma,
        dma,
        dma,
        dma,
        dma,
        dma,
        dma,
        dma((3, 2)),
        dma,
        dma((2,)),
        dma((2,)),
    ]
    x, r = pl.pallas_call(
        functools.partial(kernel, cfg),
        out_shape=(flat, flat),
        in_specs=[hbm] * 6,
        out_specs=(vmem, vmem),
        scratch_shapes=scratch,
        compiler_params=pltpu.CompilerParams(
            collective_id=0, has_side_effects=True, vmem_limit_bytes=60 * 2**20
        ),
    )(
        forcing.reshape(slots * cols, lanes),
        start_guess.reshape(slots * cols, lanes),
        mean_field,
        mode_fields,
        multi_index.T,
        jnp.asarray(codes),
    )
    return (x.reshape(slots, cols, lanes), r.reshape(slots, cols, lanes))


def solution(mesh):
    placed = (
        P("chaos", "space", None),
        P("chaos", "space", None),
        P("space", None),
        P(None, "space", None),
        P("chaos", None),
        P("chaos", None),
    )
    return jax.shard_map(
        per_device,
        mesh=mesh,
        in_specs=placed,
        out_specs=(P("chaos", "space", None), P("chaos", "space", None)),
        check_vma=False,
    )
```

```python
import functools
import math

import jax
import jax.numpy as jnp
import numpy as np
from jax import lax
from jax.experimental import pallas as pl
from jax.experimental.pallas import tpu as pltpu
from jax.sharding import PartitionSpec as P

MESH = pl.DeviceIdType.MESH
F32 = jnp.float32
DEGREE = 3
LANES = 128
PAD = 40


def term_list(modes, degree):
    def build(count, left):
        if count == 0:
            return [()]
        return [(a,) + tail for a in range(left + 1) for tail in build(count - 1, left - a)]

    return sorted(build(modes, degree), key=sum)


def code_of(term):
    return sum(m * 4**k for k, m in enumerate(term))


def kernel(
    cfg,
    f_hbm,
    x_hbm,
    mean_hbm,
    modes_hbm,
    index_hbm,
    code_hbm,
    xo_ref,
    ro_ref,
    f_ref,
    x_ref,
    mean_ref,
    modes_ref,
    index_ref,
    code_ref,
    si,
    sbx,
    sbf,
    scode,
    scoef,
    rx,
    rf,
    rcode,
    rcoef,
    pick,
    field,
    forced,
    halo,
    grad,
    flux,
    faces,
    outs,
    back,
    dot_local,
    dot_a,
    dot_b_local,
    dot_b,
    sx,
    sf,
    sc,
    sk,
    sh,
    so,
    sda,
    sdb,
    qx,
    qf,
    qc,
    qk,
    qh,
    qo,
    qda,
    qdb,
):
    slots, cols, terms, modes = cfg["slots"], cfg["cols"], cfg["terms"], cfg["modes"]
    rows = cfg["rows"]
    full = cfg["full"]
    position = {t: i for i, t in enumerate(terms)}

    space, chaos = lax.axis_index("space"), lax.axis_index("chaos")
    pair, core = space // 2, space % 2
    xx, zz = chaos // 2, chaos % 2
    lane_at = xx + zz * (3 - 2 * xx)
    member = 8 * zz + 2 * lane_at + core
    me = 16 * pair + member
    last = 127

    def device(j):
        p = (j // 2) % 8
        z = p // 4
        inner = p % 4
        x = inner + z * (3 - 2 * inner)
        return (2 * (j // 16) + j % 2, 2 * x + z)

    yy, high = pair // 2, pair % 2
    column_rank = 4 * high + 2 * zz + core
    plane_rank = 4 * yy + xx

    def in_column(r):
        return (4 * yy + 2 * (r // 4) + r % 2, 2 * xx + (r // 2) % 2)

    def in_plane(r):
        return (4 * (r // 4) + 2 * high + core, 2 * (r % 4) + zz)

    def remote(src, dst, ssem, rsem, where):
        return pltpu.make_async_remote_copy(
            src_ref=src, dst_ref=dst, send_sem=ssem, recv_sem=rsem, device_id=where, device_id_type=MESH
        )

    loads = [
        pltpu.make_async_copy(src, dst, si.at[n])
        for n, (src, dst) in enumerate(
            (
                (index_hbm, index_ref),
                (x_hbm, x_ref),
                (mean_hbm, mean_ref),
                (modes_hbm, modes_ref),
                (code_hbm, code_ref),
                (f_hbm, f_ref),
            )
        )
    ]
    for load in loads:
        load.start()

    zero8 = jnp.zeros((8, LANES), F32)
    for g in range(8):
        for c in range(2):
            rx[g, c, 32:40, :] = zero8
            rf[g, c, 32:40, :] = zero8

    @pl.when(me == 0)
    def _():
        for i in range(3):
            halo[i, 0] = jnp.zeros((full, LANES), F32)

    @pl.when(me == last)
    def _():
        for i in range(3):
            halo[i, 1] = jnp.zeros((full, LANES), F32)

    barrier = pltpu.get_barrier_semaphore()

    def greet(where):
        pl.semaphore_signal(barrier, inc=1, device_id=where, device_id_type=MESH)

    for o in range(1, 16):
        greet(in_plane((plane_rank + o) % 16))
    for o in range(1, 8):
        greet(in_column((column_rank + o) % 8))
    for dx in range(1, 4):
        for other_z, other_core in ((0, 1), (1, 0), (1, 1)):
            greet((2 * pair + (core + other_core) % 2, 2 * ((xx + dx) % 4) + (zz + other_z) % 2))
    pl.when(me > 0)(lambda: greet(device(me - 1)))
    pl.when(me < last)(lambda: greet(device(me + 1)))

    loads[0].wait()
    power = jnp.left_shift(1, 2 * lax.broadcasted_iota(jnp.int32, (modes, slots), 0)).astype(F32)
    code = jnp.sum(index_ref[...].astype(F32) * power, axis=0, keepdims=True)
    scode[...] = jnp.full((8, LANES), -1.0, F32)
    scode[:, 0:slots] = jnp.broadcast_to(code, (8, slots))

    loads[1].wait()
    greeted = 15 + 7 + 9 + jnp.where(me > 0, 1, 0) + jnp.where(me < last, 1, 0)
    pl.semaphore_wait(barrier, greeted)

    def piece(send, land, ssem, rsem, i):
        where = device(8 * space + i)
        return remote(send, land, ssem, rsem, where)

    def far_first(o):
        target_x = (xx + (2, 2, 1, 1, 3, 3, 0, 0)[o]) % 4
        return 2 * (target_x + core * (3 - 2 * target_x)) + o % 2

    def scatter(copy_of, keep, ready=None):
        for o in range(8):
            i = far_first(o)
            target = 8 * space + i
            if ready is not None:
                ready(i)
            pl.when(target != me)(lambda: copy_of(i).start())
            pl.when(target == me)(lambda: keep(i))

    own_source = (me // 8) == space

    def whole(view, ssem, rsem):
        return remote(view, view, ssem, rsem, device(me))

    def arrive(view_of, ssem, rsem):
        pl.when(own_source)(lambda: whole(view_of(7), ssem, rsem).wait_recv())
        pl.when(jnp.logical_not(own_source))(lambda: whole(view_of(8), ssem, rsem).wait_recv())

    def sent(view_of, ssem, rsem):
        pl.when(own_source)(lambda: whole(view_of(7), ssem, rsem).wait_send())
        pl.when(jnp.logical_not(own_source))(lambda: whole(view_of(8), ssem, rsem).wait_send())

    def codes_of(n):
        return rcode.at[pl.ds(0, n)]

    def x_of(n):
        return rx.at[pl.ds(0, n), :, pl.ds(0, slots)]

    def f_of(n):
        return rf.at[pl.ds(0, n), :, pl.ds(0, slots)]

    def back_of(n):
        return back.at[:, pl.ds(0, 2 * n), pl.ds(0, slots)]

    def code_copy(i):
        return piece(scode, rcode.at[chaos], sc, qc, i)

    def x_copy(i):
        return piece(
            sbx.at[pl.ds(2 * i, 2), pl.ds(0, slots)], rx.at[chaos, :, pl.ds(0, slots)], sx, qx, i
        )

    def f_copy(i):
        return piece(
            sbf.at[pl.ds(2 * i, 2), pl.ds(0, slots)], rf.at[chaos, :, pl.ds(0, slots)], sf, qf, i
        )

    def keep_code(i):
        rcode[chaos] = scode[...]

    def keep(land, send):
        def run(i):
            for c in range(2):
                land[chaos, c, 0:slots, :] = send[2 * i + c, 0:slots, :]

        return run

    def packed(src, dst):
        def run(i):
            for c in range(2):
                dst[2 * i + c, 0:slots, :] = src[pl.ds(2 * i + c, slots, stride=cols), :]

        return run

    sibling = me + 1 - 2 * core
    coef_copy = remote(scoef.at[1], rcoef, sk, qk, device(sibling))
    scatter(code_copy, keep_code)
    scatter(x_copy, keep(rx, sbx), packed(x_ref, sbx))
    loads[2].wait()
    loads[3].wait()
    mine = 2 * lane_at + core
    other = 2 * lane_at + (1 - core)
    for which, first in ((0, 2 * mine), (1, 2 * other)):
        for c in range(2):
            scoef[which, c, 8:16, :] = zero8
            scoef[which, c, 0:1, :] = mean_ref[pl.ds(first + c, 1), :]
            for k in range(modes):
                scoef[which, c, 1 + k : 2 + k, :] = modes_ref[k, pl.ds(first + c, 1), :]
    coef_copy.start()

    loads[5].wait()
    scatter(f_copy, keep(rf, sbf), packed(f_ref, sbf))

    arrive(codes_of, sc, qc)
    loads[4].wait()
    sub40 = lax.broadcasted_iota(jnp.int32, (PAD, LANES), 0)
    lane40 = lax.broadcasted_iota(jnp.int32, (PAD, LANES), 1)
    for g in range(8):
        spread = jnp.where(sub40 == lane40, rcode[g, 0:1, :], 0.0)
        placed = jnp.sum(spread, axis=1, keepdims=True)
        pick[PAD * g : PAD * (g + 1), :] = jnp.where(placed == code_ref[0:1, :], 1.0, 0.0)

    def parts(value):
        high = value.astype(jnp.bfloat16)
        rest = value - high.astype(F32)
        mid = rest.astype(jnp.bfloat16)
        low = (rest - mid.astype(F32)).astype(jnp.bfloat16)
        return [high, mid, low]

    def select(first, second, transposed):
        both = parts(first) + parts(second)
        return lax.dot_general(
            pick[...].astype(jnp.bfloat16),
            jnp.concatenate(both, axis=1),
            (((0 if transposed else 1,), (0,)), ((), ())),
            preferred_element_type=F32,
        )

    def column(result, c):
        base = 3 * LANES * c
        return (
            result[:, base : base + LANES]
            + result[:, base + LANES : base + 2 * LANES]
            + result[:, base + 2 * LANES : base + 3 * LANES]
        )

    def span(i):
        return pl.ds(0, rows if i else full)

    def halo_left(i):
        return remote(
            field.at[i, 0, span(i)], halo.at[i, 1, span(i)], sh.at[i, 0], qh.at[i, 1], device(me - 1)
        )

    def halo_right(i):
        return remote(
            field.at[i, 1, span(i)], halo.at[i, 0, span(i)], sh.at[i, 1], qh.at[i, 0], device(me + 1)
        )

    def halo_start(i):
        pl.when(me > 0)(lambda: halo_left(i).start())
        pl.when(me < last)(lambda: halo_right(i).start())

    def halo_wait(i):
        pl.when(me > 0)(lambda: halo_right(i).wait_recv())
        pl.when(me < last)(lambda: halo_left(i).wait_recv())

    def halo_sent(i):
        pl.when(me > 0)(lambda: halo_left(i).wait_send())
        pl.when(me < last)(lambda: halo_right(i).wait_send())

    coef_copy.wait_recv()
    local = core == zz
    for c in range(2):
        field[0, c, rows:full, :] = jnp.where(local, scoef[0, c], rcoef[c])

    arrive(x_of, sx, qx)
    got = select(rx[:, 0].reshape(8 * PAD, LANES), rx[:, 1].reshape(8 * PAD, LANES), True)
    for c in range(2):
        field[0, c, 0:rows, :] = column(got, c)[0:rows]

    halo_start(0)

    lane8 = lax.broadcasted_iota(jnp.int32, (8, LANES), 1)

    def back_copy(i, g):
        return remote(
            outs.at[i, g, :, pl.ds(0, slots)],
            back.at[i, pl.ds(2 * (me % 8), 2), pl.ds(0, slots)],
            so,
            qo,
            (me // 8, g),
        )

    def prepare_back(i):
        got = select(field[i + 1, 0, 0:rows, :], field[i + 1, 1, 0:rows, :], False)
        for c in range(2):
            whole = column(got, c)
            for g in range(8):
                outs[i, g, c] = whole[PAD * g : PAD * (g + 1)]

    def send_back(i):
        for o in range(8):
            g = (o + chaos) % 8
            here = jnp.logical_and(own_source, g == chaos)
            pl.when(jnp.logical_not(here))(lambda: back_copy(i, g).start())

            @pl.when(here)
            def _():
                back[i, pl.ds(2 * (me % 8), 2), 0:slots] = outs[i, g, :, 0:slots]

    def dots(which, values):
        dot_local[which] = zero8
        for n, value in enumerate(values):
            dot_local[which, n : n + 1, :] = jnp.sum(value, axis=0, keepdims=True)

    def dot_a_copy(which, o):
        return remote(
            dot_local.at[which],
            dot_a.at[which, column_rank],
            sda,
            qda.at[which],
            in_column((column_rank + o) % 8),
        )

    def dot_b_copy(which, o):
        return remote(
            dot_b_local.at[which],
            dot_b.at[which, plane_rank],
            sdb,
            qdb.at[which],
            in_plane((plane_rank + o) % 16),
        )

    def dot_a_start(which):
        for o in range(1, 8):
            dot_a_copy(which, o).start()
        dot_a[which, column_rank] = dot_local[which]

    def dot_b_start(which):
        whole(dot_a.at[which, pl.ds(0, 7)], sda, qda.at[which]).wait_recv()
        total = dot_a[which, 0]
        for m in range(1, 8):
            total = total + dot_a[which, m]
        dot_b_local[which] = total
        for o in range(1, 16):
            dot_b_copy(which, o).start()
        dot_b[which, plane_rank] = total

    def dot_total(which):
        whole(dot_b.at[which, pl.ds(0, 15)], sdb, qdb.at[which]).wait_recv()
        total = dot_b[which, 0]
        for m in range(1, 16):
            total = total + dot_b[which, m]
        return jnp.sum(total, axis=1, keepdims=True)

    halo_wait(0)
    for h in range(2):
        part = pl.ds(rows + 8 * h, 8)
        left, c0, c1, right = halo[0, 0, part], field[0, 0, part], field[0, 1, part], halo[0, 1, part]

        def up(value):
            return jnp.where(lane8 < LANES - 1, pltpu.roll(value, LANES - 1, 1), 0.0)

        kinds = [
            0.5 * (left + c0),
            0.5 * (c0 + c1),
            0.5 * (c1 + right),
            0.5 * (c0 + up(c0)),
            0.5 * (c1 + up(c1)),
            jnp.where(lane8 == 0, 0.5 * c0, 0.0),
            jnp.where(lane8 == 0, 0.5 * c1, 0.0),
            zero8,
        ]
        for n, kind in enumerate(kinds):
            faces[pl.ds(64 * h + n, 8, stride=8), :] = kind

    def gradients(i):
        if i:
            halo_wait(i)
        for b in range(rows // 8):
            part = pl.ds(8 * b, 8)
            left, u0, u1, right = halo[i, 0, part], field[i, 0, part], field[i, 1, part], halo[i, 1, part]
            up0 = jnp.where(lane8 < LANES - 1, pltpu.roll(u0, LANES - 1, 1), 0.0)
            up1 = jnp.where(lane8 < LANES - 1, pltpu.roll(u1, LANES - 1, 1), 0.0)
            kinds = [u0 - left, u1 - u0, right - u1, up0 - u0, up1 - u1]
            kinds += [jnp.where(lane8 == 0, u0, 0.0), jnp.where(lane8 == 0, u1, 0.0), zero8]
            for n, kind in enumerate(kinds):
                grad[pl.ds(64 * b + n, 8, stride=8), :] = kind

    def mixing():
        weight = [faces[8 * k : 8 * (k + 1), :] for k in range(modes + 1)]
        for s, term in enumerate(terms):
            total = weight[0] * grad[8 * s : 8 * (s + 1), :]
            for k in range(modes):
                mix = None
                for step, square in ((1, term[k] + 1), (-1, term[k])):
                    near = term[:k] + (term[k] + step,) + term[k + 1 :]
                    if near not in position:
                        continue
                    at = position[near]
                    value = grad[8 * at : 8 * (at + 1), :]
                    if square > 1:
                        value = math.sqrt(square) * value
                    mix = value if mix is None else mix + value
                if mix is not None:
                    total = total + weight[k + 1] * mix
            flux[8 * s : 8 * (s + 1), :] = total
        for s in range(len(terms), rows):
            flux[8 * s : 8 * (s + 1), :] = zero8

    def divergence(i, after):
        for b in range(rows // 8):
            kind = [flux[pl.ds(64 * b + n, 8, stride=8), :] for n in range(7)]
            part = pl.ds(8 * b, 8)
            for c in range(2):
                down = jnp.where(lane8 > 0, pltpu.roll(kind[3 + c], 1, 1), kind[5 + c])
                after(c, part, kind[c] - kind[c + 1] + down - kind[3 + c])

    gradients(0)
    mixing()
    arrive(f_of, sf, qf)
    got = select(rf[:, 0].reshape(8 * PAD, LANES), rf[:, 1].reshape(8 * PAD, LANES), True)
    for c in range(2):
        forced[c] = column(got, c)[0:rows]

    def first(c, part, value):
        field[1, c, part, :] = forced[c, part, :] - value

    divergence(0, first)
    halo_start(1)
    prepare_back(0)

    gradients(1)
    send_back(0)
    mixing()

    def second(c, part, value):
        field[2, c, part, :] = value

    divergence(1, second)
    halo_start(2)
    prepare_back(1)

    gradients(2)
    send_back(1)
    mixing()
    sums = [zero8] * 5

    def third(c, part, value):
        field[3, c, part, :] = value
        r, w = field[1, c, part, :], field[2, c, part, :]
        for n, (a, b) in enumerate(((r, r), (r, w), (w, w), (r, value), (w, value))):
            sums[n] = sums[n] + a * b

    divergence(2, third)
    dots(0, sums)
    dot_a_start(0)
    prepare_back(2)
    send_back(2)
    dot_b_start(0)
    total = dot_total(0)
    rr, rw, ww, rv, wv = (total[n : n + 1] for n in range(5))
    alpha = rr / rw
    rr1 = rr - 2.0 * alpha * rw + alpha * alpha * ww
    rar = rw - alpha * (rv + ww) + alpha * alpha * wv
    cross = 2.0 * rw - alpha * (ww + rv)
    beta = rr1 / rr
    step = rr1 / (rar + beta * cross + beta * beta * rw)

    arrive(back_of, so, qo)

    for c in range(cols):
        r0, w, v = back[0, c, 0:slots], back[1, c, 0:slots], back[2, c, 0:slots]
        x = x_ref[pl.ds(c, slots, stride=cols), :]
        xo_ref[pl.ds(c, slots, stride=cols), :] = x + (alpha + step + step * beta) * r0 - (step * alpha) * w
        r1 = r0 - alpha * w
        ro_ref[pl.ds(c, slots, stride=cols), :] = r1 - step * (w - alpha * v + beta * w)

    sent(codes_of, sc, qc)
    sent(x_of, sx, qx)
    sent(f_of, sf, qf)
    sent(back_of, so, qo)
    coef_copy.wait_send()
    for i in range(3):
        halo_sent(i)
    whole(dot_a.at[0, pl.ds(0, 7)], sda, qda.at[0]).wait_send()
    whole(dot_b.at[0, pl.ds(0, 15)], sdb, qdb.at[0]).wait_send()


def per_device(forcing, start_guess, mean_field, mode_fields, multi_index, coupled_slot):
    slots, cols, lanes = forcing.shape
    modes = mode_fields.shape[0]
    terms = term_list(modes, DEGREE)
    rows = -(-len(terms) // 8) * 8
    full = rows + 16
    wide = rows
    codes = np.full((8, wide), -2.0, np.float32)
    codes[:, : len(terms)] = [code_of(t) for t in terms]
    cfg = dict(slots=slots, cols=cols, terms=terms, modes=modes, rows=rows, full=full)
    flat = pltpu.VMEM((slots * cols, lanes), F32)
    vmem = pl.BlockSpec(memory_space=pltpu.VMEM)
    hbm = pl.BlockSpec(memory_space=pltpu.HBM)
    dma, V = pltpu.SemaphoreType.DMA, pltpu.VMEM
    scratch = [
        V((slots * cols, lanes), F32),
        V((slots * cols, lanes), F32),
        V((cols, lanes), F32),
        V((modes, cols, lanes), F32),
        V((modes, slots), jnp.int32),
        V((8, wide), F32),
        dma((6,)),
        V((cols, PAD, lanes), F32),
        V((cols, PAD, lanes), F32),
        V((8, lanes), F32),
        V((2, 2, 16, lanes), F32),
        V((8, 2, PAD, lanes), F32),
        V((8, 2, PAD, lanes), F32),
        V((8, 8, lanes), F32),
        V((2, 16, lanes), F32),
        V((8 * PAD, wide), F32),
        V((4, 2, full, lanes), F32),
        V((2, rows, lanes), F32),
        V((3, 2, full, lanes), F32),
        V((8 * rows, lanes), F32),
        V((8 * rows, lanes), F32),
        V((128, lanes), F32),
        V((3, 8, 2, PAD, lanes), F32),
        V((3, cols, PAD, lanes), F32),
        V((1, 8, lanes), F32),
        V((1, 8, 8, lanes), F32),
        V((1, 8, lanes), F32),
        V((1, 16, 8, lanes), F32),
        dma,
        dma,
        dma,
        dma,
        dma((3, 2)),
        dma,
        dma,
        dma,
        dma,
        dma,
        dma,
        dma,
        dma((3, 2)),
        dma,
        dma((1,)),
        dma((1,)),
    ]
    x, r = pl.pallas_call(
        functools.partial(kernel, cfg),
        out_shape=(flat, flat),
        in_specs=[hbm] * 6,
        out_specs=(vmem, vmem),
        scratch_shapes=scratch,
        compiler_params=pltpu.CompilerParams(
            collective_id=0, has_side_effects=True, vmem_limit_bytes=60 * 2**20
        ),
    )(
        forcing.reshape(slots * cols, lanes),
        start_guess.reshape(slots * cols, lanes),
        mean_field,
        mode_fields,
        multi_index.T,
        jnp.asarray(codes),
    )
    return (x.reshape(slots, cols, lanes), r.reshape(slots, cols, lanes))


def solution(mesh):
    placed = (
        P("chaos", "space", None),
        P("chaos", "space", None),
        P("space", None),
        P(None, "space", None),
        P("chaos", None),
        P("chaos", None),
    )
    return jax.shard_map(
        per_device,
        mesh=mesh,
        in_specs=placed,
        out_specs=(P("chaos", "space", None), P("chaos", "space", None)),
        check_vma=False,
    )
```

```python
import functools
import math

import jax
import jax.numpy as jnp
import numpy as np
from jax import lax
from jax.experimental import pallas as pl
from jax.experimental.pallas import tpu as pltpu
from jax.sharding import PartitionSpec as P

MESH = pl.DeviceIdType.MESH
F32 = jnp.float32
DEGREE = 3
LANES = 128
PAD = 40


def term_list(modes, degree):
    def build(count, left):
        if count == 0:
            return [()]
        return [(a,) + tail for a in range(left + 1) for tail in build(count - 1, left - a)]

    return sorted(build(modes, degree), key=sum)


def code_of(term):
    return sum(m * 4**k for k, m in enumerate(term))


def kernel(
    cfg,
    f_hbm,
    x_hbm,
    mean_hbm,
    modes_hbm,
    index_hbm,
    code_hbm,
    xo_ref,
    ro_ref,
    f_ref,
    x_ref,
    mean_ref,
    modes_ref,
    index_ref,
    code_ref,
    si,
    sbx,
    sbf,
    scode,
    scoef,
    rx,
    rf,
    rcode,
    rcoef,
    pick,
    field,
    forced,
    halo,
    grad,
    flux,
    faces,
    outs,
    back,
    dot_local,
    dot_a,
    dot_b_local,
    dot_b,
    sx,
    sf,
    sc,
    sk,
    sh,
    so,
    sda,
    sdb,
    qx,
    qf,
    qc,
    qk,
    qh,
    qo,
    qda,
    qdb,
):
    slots, cols, terms, modes = cfg["slots"], cfg["cols"], cfg["terms"], cfg["modes"]
    rows = cfg["rows"]
    full = cfg["full"]
    position = {t: i for i, t in enumerate(terms)}

    space, chaos = lax.axis_index("space"), lax.axis_index("chaos")
    pair, core = space // 2, space % 2
    xx, zz = chaos // 2, chaos % 2
    lane_at = xx + zz * (3 - 2 * xx)
    member = 8 * zz + 2 * lane_at + core
    me = 16 * pair + member
    last = 127

    def device(j):
        p = (j // 2) % 8
        z = p // 4
        inner = p % 4
        x = inner + z * (3 - 2 * inner)
        return (2 * (j // 16) + j % 2, 2 * x + z)

    yy, high = pair // 2, pair % 2
    column_rank = 4 * high + 2 * zz + core
    plane_rank = 4 * yy + xx

    def in_column(r):
        return (4 * yy + 2 * (r // 4) + r % 2, 2 * xx + (r // 2) % 2)

    def in_plane(r):
        return (4 * (r // 4) + 2 * high + core, 2 * (r % 4) + zz)

    def remote(src, dst, ssem, rsem, where):
        return pltpu.make_async_remote_copy(
            src_ref=src, dst_ref=dst, send_sem=ssem, recv_sem=rsem, device_id=where, device_id_type=MESH
        )

    loads = [
        pltpu.make_async_copy(src, dst, si.at[n])
        for n, (src, dst) in enumerate(
            (
                (index_hbm, index_ref),
                (x_hbm, x_ref),
                (mean_hbm, mean_ref),
                (modes_hbm, modes_ref),
                (code_hbm, code_ref),
                (f_hbm, f_ref),
            )
        )
    ]
    for load in loads:
        load.start()

    zero8 = jnp.zeros((8, LANES), F32)
    for g in range(8):
        for c in range(2):
            rx[g, c, 32:40, :] = zero8
            rf[g, c, 32:40, :] = zero8

    @pl.when(me == 0)
    def _():
        for i in range(3):
            halo[i, 0] = jnp.zeros((full, LANES), F32)

    @pl.when(me == last)
    def _():
        for i in range(3):
            halo[i, 1] = jnp.zeros((full, LANES), F32)

    barrier = pltpu.get_barrier_semaphore()

    def greet(where):
        pl.semaphore_signal(barrier, inc=1, device_id=where, device_id_type=MESH)

    for o in range(1, 16):
        greet(in_plane((plane_rank + o) % 16))
    for o in range(1, 8):
        greet(in_column((column_rank + o) % 8))
    for dx in range(1, 4):
        for other_z, other_core in ((0, 1), (1, 0), (1, 1)):
            greet((2 * pair + (core + other_core) % 2, 2 * ((xx + dx) % 4) + (zz + other_z) % 2))
    pl.when(me > 0)(lambda: greet(device(me - 1)))
    pl.when(me < last)(lambda: greet(device(me + 1)))

    loads[0].wait()
    power = jnp.left_shift(1, 2 * lax.broadcasted_iota(jnp.int32, (modes, slots), 0)).astype(F32)
    code = jnp.sum(index_ref[...].astype(F32) * power, axis=0, keepdims=True)
    scode[...] = jnp.full((8, LANES), -1.0, F32)
    scode[:, 0:slots] = jnp.broadcast_to(code, (8, slots))

    loads[1].wait()
    greeted = 15 + 7 + 9 + jnp.where(me > 0, 1, 0) + jnp.where(me < last, 1, 0)
    pl.semaphore_wait(barrier, greeted)

    def piece(send, land, ssem, rsem, i):
        where = device(8 * space + i)
        return remote(send, land, ssem, rsem, where)

    def far_first(o):
        target_x = (xx + (2, 2, 1, 1, 3, 3, 0, 0)[o]) % 4
        return 2 * (target_x + core * (3 - 2 * target_x)) + o % 2

    def scatter(copy_of, keep, ready=None):
        for o in range(8):
            i = far_first(o)
            target = 8 * space + i
            if ready is not None:
                ready(i)
            pl.when(target != me)(lambda: copy_of(i).start())
            pl.when(target == me)(lambda: keep(i))

    own_source = (me // 8) == space

    def whole(view, ssem, rsem):
        return remote(view, view, ssem, rsem, device(me))

    def arrive(view_of, ssem, rsem):
        pl.when(own_source)(lambda: whole(view_of(7), ssem, rsem).wait_recv())
        pl.when(jnp.logical_not(own_source))(lambda: whole(view_of(8), ssem, rsem).wait_recv())

    def sent(view_of, ssem, rsem):
        pl.when(own_source)(lambda: whole(view_of(7), ssem, rsem).wait_send())
        pl.when(jnp.logical_not(own_source))(lambda: whole(view_of(8), ssem, rsem).wait_send())

    def codes_of(n):
        return rcode.at[pl.ds(0, n)]

    def x_of(n):
        return rx.at[pl.ds(0, n), :, pl.ds(0, slots)]

    def f_of(n):
        return rf.at[pl.ds(0, n), :, pl.ds(0, slots)]

    def back_of(n):
        return back.at[:, pl.ds(0, 2 * n), pl.ds(0, slots)]

    def code_copy(i):
        return piece(scode, rcode.at[chaos], sc, qc, i)

    def x_copy(i):
        return piece(
            sbx.at[pl.ds(2 * i, 2), pl.ds(0, slots)], rx.at[chaos, :, pl.ds(0, slots)], sx, qx, i
        )

    def f_copy(i):
        return piece(
            sbf.at[pl.ds(2 * i, 2), pl.ds(0, slots)], rf.at[chaos, :, pl.ds(0, slots)], sf, qf, i
        )

    def keep_code(i):
        rcode[chaos] = scode[...]

    def keep(land, send):
        def run(i):
            for c in range(2):
                land[chaos, c, 0:slots, :] = send[2 * i + c, 0:slots, :]

        return run

    def packed(src, dst):
        def run(i):
            for c in range(2):
                dst[2 * i + c, 0:slots, :] = src[pl.ds(2 * i + c, slots, stride=cols), :]

        return run

    sibling = me + 1 - 2 * core
    coef_copy = remote(scoef.at[1], rcoef, sk, qk, device(sibling))
    scatter(code_copy, keep_code)
    scatter(x_copy, keep(rx, sbx), packed(x_ref, sbx))
    loads[2].wait()
    loads[3].wait()
    mine = 2 * lane_at + core
    other = 2 * lane_at + (1 - core)
    for which, first in ((0, 2 * mine), (1, 2 * other)):
        for c in range(2):
            scoef[which, c, 8:16, :] = zero8
            scoef[which, c, 0:1, :] = mean_ref[pl.ds(first + c, 1), :]
            for k in range(modes):
                scoef[which, c, 1 + k : 2 + k, :] = modes_ref[k, pl.ds(first + c, 1), :]
    coef_copy.start()

    loads[5].wait()
    scatter(f_copy, keep(rf, sbf), packed(f_ref, sbf))

    arrive(codes_of, sc, qc)
    loads[4].wait()
    sub40 = lax.broadcasted_iota(jnp.int32, (PAD, LANES), 0)
    lane40 = lax.broadcasted_iota(jnp.int32, (PAD, LANES), 1)
    for g in range(8):
        spread = jnp.where(sub40 == lane40, rcode[g, 0:1, :], 0.0)
        placed = jnp.sum(spread, axis=1, keepdims=True)
        pick[PAD * g : PAD * (g + 1), :] = jnp.where(placed == code_ref[0:1, :], 1.0, 0.0)

    def parts(value):
        high = value.astype(jnp.bfloat16)
        rest = value - high.astype(F32)
        mid = rest.astype(jnp.bfloat16)
        low = (rest - mid.astype(F32)).astype(jnp.bfloat16)
        return [high, mid, low]

    def select(first, second, transposed):
        both = parts(first) + parts(second)
        return lax.dot_general(
            pick[...].astype(jnp.bfloat16),
            jnp.concatenate(both, axis=1),
            (((0 if transposed else 1,), (0,)), ((), ())),
            preferred_element_type=F32,
        )

    def column(result, c):
        base = 3 * LANES * c
        return (
            result[:, base : base + LANES]
            + result[:, base + LANES : base + 2 * LANES]
            + result[:, base + 2 * LANES : base + 3 * LANES]
        )

    def span(i):
        return pl.ds(0, rows if i else full)

    def halo_left(i):
        return remote(
            field.at[i, 0, span(i)], halo.at[i, 1, span(i)], sh.at[i, 0], qh.at[i, 1], device(me - 1)
        )

    def halo_right(i):
        return remote(
            field.at[i, 1, span(i)], halo.at[i, 0, span(i)], sh.at[i, 1], qh.at[i, 0], device(me + 1)
        )

    def halo_start(i):
        pl.when(me > 0)(lambda: halo_left(i).start())
        pl.when(me < last)(lambda: halo_right(i).start())

    def halo_wait(i):
        pl.when(me > 0)(lambda: halo_right(i).wait_recv())
        pl.when(me < last)(lambda: halo_left(i).wait_recv())

    def halo_sent(i):
        pl.when(me > 0)(lambda: halo_left(i).wait_send())
        pl.when(me < last)(lambda: halo_right(i).wait_send())

    coef_copy.wait_recv()
    local = core == zz
    for c in range(2):
        field[0, c, rows:full, :] = jnp.where(local, scoef[0, c], rcoef[c])

    arrive(x_of, sx, qx)
    got = select(rx[:, 0].reshape(8 * PAD, LANES), rx[:, 1].reshape(8 * PAD, LANES), True)
    for c in range(2):
        field[0, c, 0:rows, :] = column(got, c)[0:rows]

    halo_start(0)

    lane8 = lax.broadcasted_iota(jnp.int32, (8, LANES), 1)

    def back_copy(i, g):
        return remote(
            outs.at[i, g, :, pl.ds(0, slots)],
            back.at[i, pl.ds(2 * (me % 8), 2), pl.ds(0, slots)],
            so,
            qo,
            (me // 8, g),
        )

    def prepare_back(i):
        got = select(field[i + 1, 0, 0:rows, :], field[i + 1, 1, 0:rows, :], False)
        for c in range(2):
            whole = column(got, c)
            for g in range(8):
                outs[i, g, c] = whole[PAD * g : PAD * (g + 1)]

    def send_back(i):
        for o in range(8):
            g = (o + chaos) % 8
            here = jnp.logical_and(own_source, g == chaos)
            pl.when(jnp.logical_not(here))(lambda: back_copy(i, g).start())

            @pl.when(here)
            def _():
                back[i, pl.ds(2 * (me % 8), 2), 0:slots] = outs[i, g, :, 0:slots]

    def dots(which, values):
        dot_local[which] = zero8
        for n, value in enumerate(values):
            dot_local[which, n : n + 1, :] = jnp.sum(value, axis=0, keepdims=True)

    def dot_a_copy(which, o):
        return remote(
            dot_local.at[which],
            dot_a.at[which, column_rank],
            sda,
            qda.at[which],
            in_column((column_rank + o) % 8),
        )

    def dot_b_copy(which, o):
        return remote(
            dot_b_local.at[which],
            dot_b.at[which, plane_rank],
            sdb,
            qdb.at[which],
            in_plane((plane_rank + o) % 16),
        )

    def dot_a_start(which):
        for o in range(1, 8):
            dot_a_copy(which, o).start()
        dot_a[which, column_rank] = dot_local[which]

    def dot_b_start(which):
        whole(dot_a.at[which, pl.ds(0, 7)], sda, qda.at[which]).wait_recv()
        total = dot_a[which, 0]
        for m in range(1, 8):
            total = total + dot_a[which, m]
        dot_b_local[which] = total
        for o in range(1, 16):
            dot_b_copy(which, o).start()
        dot_b[which, plane_rank] = total

    def dot_total(which):
        whole(dot_b.at[which, pl.ds(0, 15)], sdb, qdb.at[which]).wait_recv()
        total = dot_b[which, 0]
        for m in range(1, 16):
            total = total + dot_b[which, m]
        return jnp.sum(total, axis=1, keepdims=True)

    halo_wait(0)
    for h in range(2):
        part = pl.ds(rows + 8 * h, 8)
        left, c0, c1, right = halo[0, 0, part], field[0, 0, part], field[0, 1, part], halo[0, 1, part]

        def up(value):
            return jnp.where(lane8 < LANES - 1, pltpu.roll(value, LANES - 1, 1), 0.0)

        kinds = [
            0.5 * (left + c0),
            0.5 * (c0 + c1),
            0.5 * (c1 + right),
            0.5 * (c0 + up(c0)),
            0.5 * (c1 + up(c1)),
            jnp.where(lane8 == 0, 0.5 * c0, 0.0),
            jnp.where(lane8 == 0, 0.5 * c1, 0.0),
            zero8,
        ]
        for n, kind in enumerate(kinds):
            faces[pl.ds(64 * h + n, 8, stride=8), :] = kind

    def gradients(i):
        if i:
            halo_wait(i)
        for b in range(rows // 8):
            part = pl.ds(8 * b, 8)
            left, u0, u1, right = halo[i, 0, part], field[i, 0, part], field[i, 1, part], halo[i, 1, part]
            up0 = jnp.where(lane8 < LANES - 1, pltpu.roll(u0, LANES - 1, 1), 0.0)
            up1 = jnp.where(lane8 < LANES - 1, pltpu.roll(u1, LANES - 1, 1), 0.0)
            kinds = [u0 - left, u1 - u0, right - u1, up0 - u0, up1 - u1]
            kinds += [jnp.where(lane8 == 0, u0, 0.0), jnp.where(lane8 == 0, u1, 0.0), zero8]
            for n, kind in enumerate(kinds):
                grad[pl.ds(64 * b + n, 8, stride=8), :] = kind

    def mixing():
        weight = [faces[8 * k : 8 * (k + 1), :] for k in range(modes + 1)]
        for s, term in enumerate(terms):
            total = weight[0] * grad[8 * s : 8 * (s + 1), :]
            for k in range(modes):
                mix = None
                for step, square in ((1, term[k] + 1), (-1, term[k])):
                    near = term[:k] + (term[k] + step,) + term[k + 1 :]
                    if near not in position:
                        continue
                    at = position[near]
                    value = grad[8 * at : 8 * (at + 1), :]
                    if square > 1:
                        value = math.sqrt(square) * value
                    mix = value if mix is None else mix + value
                if mix is not None:
                    total = total + weight[k + 1] * mix
            flux[8 * s : 8 * (s + 1), :] = total
        for s in range(len(terms), rows):
            flux[8 * s : 8 * (s + 1), :] = zero8

    def divergence(i, after):
        for b in range(rows // 8):
            kind = [flux[pl.ds(64 * b + n, 8, stride=8), :] for n in range(7)]
            part = pl.ds(8 * b, 8)
            for c in range(2):
                down = jnp.where(lane8 > 0, pltpu.roll(kind[3 + c], 1, 1), kind[5 + c])
                after(c, part, kind[c] - kind[c + 1] + down - kind[3 + c])

    gradients(0)
    mixing()
    arrive(f_of, sf, qf)
    got = select(rf[:, 0].reshape(8 * PAD, LANES), rf[:, 1].reshape(8 * PAD, LANES), True)
    for c in range(2):
        forced[c] = column(got, c)[0:rows]

    def first(c, part, value):
        field[1, c, part, :] = forced[c, part, :] - value

    divergence(0, first)
    halo_start(1)
    prepare_back(0)

    gradients(1)
    send_back(0)
    mixing()

    def second(c, part, value):
        field[2, c, part, :] = value

    divergence(1, second)
    halo_start(2)
    prepare_back(1)

    gradients(2)
    send_back(1)
    mixing()
    sums = [zero8] * 5

    def third(c, part, value):
        field[3, c, part, :] = value
        r, w = field[1, c, part, :], field[2, c, part, :]
        for n, (a, b) in enumerate(((r, r), (r, w), (w, w), (r, value), (w, value))):
            sums[n] = sums[n] + a * b

    divergence(2, third)
    dots(0, sums)
    dot_a_start(0)
    prepare_back(2)
    dot_b_start(0)
    send_back(2)
    total = dot_total(0)
    rr, rw, ww, rv, wv = (total[n : n + 1] for n in range(5))
    alpha = rr / rw
    rr1 = rr - 2.0 * alpha * rw + alpha * alpha * ww
    rar = rw - alpha * (rv + ww) + alpha * alpha * wv
    cross = 2.0 * rw - alpha * (ww + rv)
    beta = rr1 / rr
    step = rr1 / (rar + beta * cross + beta * beta * rw)

    arrive(back_of, so, qo)

    for c in range(cols):
        r0, w, v = back[0, c, 0:slots], back[1, c, 0:slots], back[2, c, 0:slots]
        x = x_ref[pl.ds(c, slots, stride=cols), :]
        xo_ref[pl.ds(c, slots, stride=cols), :] = x + (alpha + step + step * beta) * r0 - (step * alpha) * w
        r1 = r0 - alpha * w
        ro_ref[pl.ds(c, slots, stride=cols), :] = r1 - step * (w - alpha * v + beta * w)

    sent(codes_of, sc, qc)
    sent(x_of, sx, qx)
    sent(f_of, sf, qf)
    sent(back_of, so, qo)
    coef_copy.wait_send()
    for i in range(3):
        halo_sent(i)
    whole(dot_a.at[0, pl.ds(0, 7)], sda, qda.at[0]).wait_send()
    whole(dot_b.at[0, pl.ds(0, 15)], sdb, qdb.at[0]).wait_send()


def per_device(forcing, start_guess, mean_field, mode_fields, multi_index, coupled_slot):
    slots, cols, lanes = forcing.shape
    modes = mode_fields.shape[0]
    terms = term_list(modes, DEGREE)
    rows = -(-len(terms) // 8) * 8
    full = rows + 16
    wide = rows
    codes = np.full((8, wide), -2.0, np.float32)
    codes[:, : len(terms)] = [code_of(t) for t in terms]
    cfg = dict(slots=slots, cols=cols, terms=terms, modes=modes, rows=rows, full=full)
    flat = pltpu.VMEM((slots * cols, lanes), F32)
    vmem = pl.BlockSpec(memory_space=pltpu.VMEM)
    hbm = pl.BlockSpec(memory_space=pltpu.HBM)
    dma, V = pltpu.SemaphoreType.DMA, pltpu.VMEM
    scratch = [
        V((slots * cols, lanes), F32),
        V((slots * cols, lanes), F32),
        V((cols, lanes), F32),
        V((modes, cols, lanes), F32),
        V((modes, slots), jnp.int32),
        V((8, wide), F32),
        dma((6,)),
        V((cols, PAD, lanes), F32),
        V((cols, PAD, lanes), F32),
        V((8, lanes), F32),
        V((2, 2, 16, lanes), F32),
        V((8, 2, PAD, lanes), F32),
        V((8, 2, PAD, lanes), F32),
        V((8, 8, lanes), F32),
        V((2, 16, lanes), F32),
        V((8 * PAD, wide), F32),
        V((4, 2, full, lanes), F32),
        V((2, rows, lanes), F32),
        V((3, 2, full, lanes), F32),
        V((8 * rows, lanes), F32),
        V((8 * rows, lanes), F32),
        V((128, lanes), F32),
        V((3, 8, 2, PAD, lanes), F32),
        V((3, cols, PAD, lanes), F32),
        V((1, 8, lanes), F32),
        V((1, 8, 8, lanes), F32),
        V((1, 8, lanes), F32),
        V((1, 16, 8, lanes), F32),
        dma,
        dma,
        dma,
        dma,
        dma((3, 2)),
        dma,
        dma,
        dma,
        dma,
        dma,
        dma,
        dma,
        dma((3, 2)),
        dma,
        dma((1,)),
        dma((1,)),
    ]
    x, r = pl.pallas_call(
        functools.partial(kernel, cfg),
        out_shape=(flat, flat),
        in_specs=[hbm] * 6,
        out_specs=(vmem, vmem),
        scratch_shapes=scratch,
        compiler_params=pltpu.CompilerParams(
            collective_id=0, has_side_effects=True, vmem_limit_bytes=60 * 2**20
        ),
    )(
        forcing.reshape(slots * cols, lanes),
        start_guess.reshape(slots * cols, lanes),
        mean_field,
        mode_fields,
        multi_index.T,
        jnp.asarray(codes),
    )
    return (x.reshape(slots, cols, lanes), r.reshape(slots, cols, lanes))


def solution(mesh):
    placed = (
        P("chaos", "space", None),
        P("chaos", "space", None),
        P("space", None),
        P(None, "space", None),
        P("chaos", None),
        P("chaos", None),
    )
    return jax.shard_map(
        per_device,
        mesh=mesh,
        in_specs=placed,
        out_specs=(P("chaos", "space", None), P("chaos", "space", None)),
        check_vma=False,
    )
```

```python
import functools
import math

import jax
import jax.numpy as jnp
import numpy as np
from jax import lax
from jax.experimental import pallas as pl
from jax.experimental.pallas import tpu as pltpu
from jax.sharding import PartitionSpec as P

MESH = pl.DeviceIdType.MESH
F32 = jnp.float32
DEGREE = 3
LANES = 128
PAD = 40


def term_list(modes, degree):
    def build(count, left):
        if count == 0:
            return [()]
        return [(a,) + tail for a in range(left + 1) for tail in build(count - 1, left - a)]

    return sorted(build(modes, degree), key=sum)


def code_of(term):
    return sum(m * 4**k for k, m in enumerate(term))


def kernel(
    cfg,
    f_hbm,
    x_hbm,
    mean_hbm,
    modes_hbm,
    index_hbm,
    code_hbm,
    xo_ref,
    ro_ref,
    f_ref,
    x_ref,
    mean_ref,
    modes_ref,
    index_ref,
    code_ref,
    si,
    sbx,
    sbf,
    scode,
    scoef,
    rx,
    rf,
    rcode,
    rcoef,
    pick,
    field,
    forced,
    halo,
    grad,
    flux,
    faces,
    outs,
    back,
    dot_local,
    dot_a,
    dot_b_local,
    dot_b,
    sx,
    sf,
    sc,
    sk,
    sh,
    so,
    sda,
    sdb,
    qx,
    qf,
    qc,
    qk,
    qh,
    qo,
    qda,
    qdb,
):
    slots, cols, terms, modes = cfg["slots"], cfg["cols"], cfg["terms"], cfg["modes"]
    rows = cfg["rows"]
    full = cfg["full"]
    position = {t: i for i, t in enumerate(terms)}

    space, chaos = lax.axis_index("space"), lax.axis_index("chaos")
    pair, core = space // 2, space % 2
    xx, zz = chaos // 2, chaos % 2
    lane_at = xx + zz * (3 - 2 * xx)
    member = 8 * zz + 2 * lane_at + core
    me = 16 * pair + member
    last = 127

    def device(j):
        p = (j // 2) % 8
        z = p // 4
        inner = p % 4
        x = inner + z * (3 - 2 * inner)
        return (2 * (j // 16) + j % 2, 2 * x + z)

    yy, high = pair // 2, pair % 2
    column_rank = 4 * high + 2 * zz + core
    plane_rank = 4 * yy + xx

    def in_column(r):
        return (4 * yy + 2 * (r // 4) + r % 2, 2 * xx + (r // 2) % 2)

    def in_plane(r):
        return (4 * (r // 4) + 2 * high + core, 2 * (r % 4) + zz)

    def remote(src, dst, ssem, rsem, where):
        return pltpu.make_async_remote_copy(
            src_ref=src, dst_ref=dst, send_sem=ssem, recv_sem=rsem, device_id=where, device_id_type=MESH
        )

    loads = [
        pltpu.make_async_copy(src, dst, si.at[n])
        for n, (src, dst) in enumerate(
            (
                (index_hbm, index_ref),
                (x_hbm, x_ref),
                (mean_hbm, mean_ref),
                (modes_hbm, modes_ref),
                (code_hbm, code_ref),
                (f_hbm, f_ref),
            )
        )
    ]
    for load in loads:
        load.start()

    zero8 = jnp.zeros((8, LANES), F32)
    for g in range(8):
        for c in range(2):
            rx[g, c, 32:40, :] = zero8
            rf[g, c, 32:40, :] = zero8

    @pl.when(me == 0)
    def _():
        for i in range(3):
            halo[i, 0] = jnp.zeros((full, LANES), F32)

    @pl.when(me == last)
    def _():
        for i in range(3):
            halo[i, 1] = jnp.zeros((full, LANES), F32)

    barrier = pltpu.get_barrier_semaphore()

    def greet(where):
        pl.semaphore_signal(barrier, inc=1, device_id=where, device_id_type=MESH)

    for o in range(1, 16):
        greet(in_plane((plane_rank + o) % 16))
    for o in range(1, 8):
        greet(in_column((column_rank + o) % 8))
    for dx in range(1, 4):
        for other_z, other_core in ((0, 1), (1, 0), (1, 1)):
            greet((2 * pair + (core + other_core) % 2, 2 * ((xx + dx) % 4) + (zz + other_z) % 2))
    pl.when(me > 0)(lambda: greet(device(me - 1)))
    pl.when(me < last)(lambda: greet(device(me + 1)))

    loads[0].wait()
    power = jnp.left_shift(1, 2 * lax.broadcasted_iota(jnp.int32, (modes, slots), 0)).astype(F32)
    code = jnp.sum(index_ref[...].astype(F32) * power, axis=0, keepdims=True)
    scode[...] = jnp.full((8, LANES), -1.0, F32)
    scode[:, 0:slots] = jnp.broadcast_to(code, (8, slots))

    loads[1].wait()
    greeted = 15 + 7 + 9 + jnp.where(me > 0, 1, 0) + jnp.where(me < last, 1, 0)
    pl.semaphore_wait(barrier, greeted)

    def piece(send, land, ssem, rsem, i):
        where = device(8 * space + i)
        return remote(send, land, ssem, rsem, where)

    def far_first(o):
        target_x = (xx + (2, 2, 1, 1, 3, 3, 0, 0)[o]) % 4
        return 2 * (target_x + core * (3 - 2 * target_x)) + o % 2

    def scatter(copy_of, keep, ready=None):
        for o in range(8):
            i = far_first(o)
            target = 8 * space + i
            if ready is not None:
                ready(i)
            pl.when(target != me)(lambda: copy_of(i).start())
            pl.when(target == me)(lambda: keep(i))

    own_source = (me // 8) == space

    def whole(view, ssem, rsem):
        return remote(view, view, ssem, rsem, device(me))

    def arrive(view_of, ssem, rsem):
        pl.when(own_source)(lambda: whole(view_of(7), ssem, rsem).wait_recv())
        pl.when(jnp.logical_not(own_source))(lambda: whole(view_of(8), ssem, rsem).wait_recv())

    def sent(view_of, ssem, rsem):
        pl.when(own_source)(lambda: whole(view_of(7), ssem, rsem).wait_send())
        pl.when(jnp.logical_not(own_source))(lambda: whole(view_of(8), ssem, rsem).wait_send())

    def codes_of(n):
        return rcode.at[pl.ds(0, n)]

    def x_of(n):
        return rx.at[pl.ds(0, n), :, pl.ds(0, slots)]

    def f_of(n):
        return rf.at[pl.ds(0, n), :, pl.ds(0, slots)]

    def back_of(n):
        return back.at[:, pl.ds(0, 2 * n), pl.ds(0, slots)]

    def code_copy(i):
        return piece(scode, rcode.at[chaos], sc, qc, i)

    def x_copy(i):
        return piece(
            sbx.at[pl.ds(2 * i, 2), pl.ds(0, slots)], rx.at[chaos, :, pl.ds(0, slots)], sx, qx, i
        )

    def f_copy(i):
        return piece(
            sbf.at[pl.ds(2 * i, 2), pl.ds(0, slots)], rf.at[chaos, :, pl.ds(0, slots)], sf, qf, i
        )

    def keep_code(i):
        rcode[chaos] = scode[...]

    def keep(land, send):
        def run(i):
            for c in range(2):
                land[chaos, c, 0:slots, :] = send[2 * i + c, 0:slots, :]

        return run

    def packed(src, dst):
        def run(i):
            for c in range(2):
                dst[2 * i + c, 0:slots, :] = src[pl.ds(2 * i + c, slots, stride=cols), :]

        return run

    sibling = me + 1 - 2 * core
    coef_copy = remote(scoef.at[1], rcoef, sk, qk, device(sibling))
    scatter(code_copy, keep_code)
    scatter(x_copy, keep(rx, sbx), packed(x_ref, sbx))
    loads[2].wait()
    loads[3].wait()
    mine = 2 * lane_at + core
    other = 2 * lane_at + (1 - core)
    for which, first in ((0, 2 * mine), (1, 2 * other)):
        for c in range(2):
            scoef[which, c, 8:16, :] = zero8
            scoef[which, c, 0:1, :] = mean_ref[pl.ds(first + c, 1), :]
            for k in range(modes):
                scoef[which, c, 1 + k : 2 + k, :] = modes_ref[k, pl.ds(first + c, 1), :]
    coef_copy.start()

    loads[5].wait()
    scatter(f_copy, keep(rf, sbf), packed(f_ref, sbf))

    arrive(codes_of, sc, qc)
    loads[4].wait()
    sub40 = lax.broadcasted_iota(jnp.int32, (PAD, LANES), 0)
    lane40 = lax.broadcasted_iota(jnp.int32, (PAD, LANES), 1)
    for g in range(8):
        spread = jnp.where(sub40 == lane40, rcode[g, 0:1, :], 0.0)
        placed = jnp.sum(spread, axis=1, keepdims=True)
        pick[PAD * g : PAD * (g + 1), :] = jnp.where(placed == code_ref[0:1, :], 1.0, 0.0)

    def parts(value):
        high = value.astype(jnp.bfloat16)
        rest = value - high.astype(F32)
        mid = rest.astype(jnp.bfloat16)
        low = (rest - mid.astype(F32)).astype(jnp.bfloat16)
        return [high, mid, low]

    def select(first, second, transposed):
        both = parts(first) + parts(second)
        return lax.dot_general(
            pick[...].astype(jnp.bfloat16),
            jnp.concatenate(both, axis=1),
            (((0 if transposed else 1,), (0,)), ((), ())),
            preferred_element_type=F32,
        )

    def column(result, c):
        base = 3 * LANES * c
        return (
            result[:, base : base + LANES]
            + result[:, base + LANES : base + 2 * LANES]
            + result[:, base + 2 * LANES : base + 3 * LANES]
        )

    def span(i):
        return pl.ds(0, rows if i else full)

    def halo_left(i):
        return remote(
            field.at[i, 0, span(i)], halo.at[i, 1, span(i)], sh.at[i, 0], qh.at[i, 1], device(me - 1)
        )

    def halo_right(i):
        return remote(
            field.at[i, 1, span(i)], halo.at[i, 0, span(i)], sh.at[i, 1], qh.at[i, 0], device(me + 1)
        )

    def halo_start(i):
        pl.when(me > 0)(lambda: halo_left(i).start())
        pl.when(me < last)(lambda: halo_right(i).start())

    def halo_wait(i):
        pl.when(me > 0)(lambda: halo_right(i).wait_recv())
        pl.when(me < last)(lambda: halo_left(i).wait_recv())

    def halo_sent(i):
        pl.when(me > 0)(lambda: halo_left(i).wait_send())
        pl.when(me < last)(lambda: halo_right(i).wait_send())

    coef_copy.wait_recv()
    local = core == zz
    for c in range(2):
        field[0, c, rows:full, :] = jnp.where(local, scoef[0, c], rcoef[c])

    arrive(x_of, sx, qx)
    got = select(rx[:, 0].reshape(8 * PAD, LANES), rx[:, 1].reshape(8 * PAD, LANES), True)
    for c in range(2):
        field[0, c, 0:rows, :] = column(got, c)[0:rows]

    halo_start(0)

    lane8 = lax.broadcasted_iota(jnp.int32, (8, LANES), 1)

    def back_copy(i, g):
        return remote(
            outs.at[i, g, :, pl.ds(0, slots)],
            back.at[i, pl.ds(2 * (me % 8), 2), pl.ds(0, slots)],
            so,
            qo,
            (me // 8, g),
        )

    def prepare_back(i):
        got = select(field[i + 1, 0, 0:rows, :], field[i + 1, 1, 0:rows, :], False)
        for c in range(2):
            whole = column(got, c)
            for g in range(8):
                outs[i, g, c] = whole[PAD * g : PAD * (g + 1)]

    def send_back(i):
        for o in range(8):
            g = (o + chaos) % 8
            here = jnp.logical_and(own_source, g == chaos)
            pl.when(jnp.logical_not(here))(lambda: back_copy(i, g).start())

            @pl.when(here)
            def _():
                back[i, pl.ds(2 * (me % 8), 2), 0:slots] = outs[i, g, :, 0:slots]

    def dots(which, values):
        dot_local[which] = zero8
        for n, value in enumerate(values):
            dot_local[which, n : n + 1, :] = jnp.sum(value, axis=0, keepdims=True)

    def dot_a_copy(which, o):
        return remote(
            dot_local.at[which],
            dot_a.at[which, column_rank],
            sda,
            qda.at[which],
            in_column((column_rank + o) % 8),
        )

    def dot_b_copy(which, o):
        return remote(
            dot_b_local.at[which],
            dot_b.at[which, plane_rank],
            sdb,
            qdb.at[which],
            in_plane((plane_rank + o) % 16),
        )

    def dot_a_start(which):
        for o in range(1, 8):
            dot_a_copy(which, o).start()
        dot_a[which, column_rank] = dot_local[which]

    def dot_b_start(which):
        whole(dot_a.at[which, pl.ds(0, 7)], sda, qda.at[which]).wait_recv()
        total = dot_a[which, 0]
        for m in range(1, 8):
            total = total + dot_a[which, m]
        dot_b_local[which] = total
        for o in range(1, 16):
            dot_b_copy(which, o).start()
        dot_b[which, plane_rank] = total

    def dot_total(which):
        whole(dot_b.at[which, pl.ds(0, 15)], sdb, qdb.at[which]).wait_recv()
        total = dot_b[which, 0]
        for m in range(1, 16):
            total = total + dot_b[which, m]
        return jnp.sum(total, axis=1, keepdims=True)

    halo_wait(0)
    for h in range(2):
        part = pl.ds(rows + 8 * h, 8)
        left, c0, c1, right = halo[0, 0, part], field[0, 0, part], field[0, 1, part], halo[0, 1, part]

        def up(value):
            return jnp.where(lane8 < LANES - 1, pltpu.roll(value, LANES - 1, 1), 0.0)

        kinds = [
            0.5 * (left + c0),
            0.5 * (c0 + c1),
            0.5 * (c1 + right),
            0.5 * (c0 + up(c0)),
            0.5 * (c1 + up(c1)),
            jnp.where(lane8 == 0, 0.5 * c0, 0.0),
            jnp.where(lane8 == 0, 0.5 * c1, 0.0),
            zero8,
        ]
        for n, kind in enumerate(kinds):
            faces[pl.ds(64 * h + n, 8, stride=8), :] = kind

    def gradients(i):
        if i:
            halo_wait(i)
        for b in range(rows // 8):
            part = pl.ds(8 * b, 8)
            left, u0, u1, right = halo[i, 0, part], field[i, 0, part], field[i, 1, part], halo[i, 1, part]
            up0 = jnp.where(lane8 < LANES - 1, pltpu.roll(u0, LANES - 1, 1), 0.0)
            up1 = jnp.where(lane8 < LANES - 1, pltpu.roll(u1, LANES - 1, 1), 0.0)
            kinds = [u0 - left, u1 - u0, right - u1, up0 - u0, up1 - u1]
            kinds += [jnp.where(lane8 == 0, u0, 0.0), jnp.where(lane8 == 0, u1, 0.0), zero8]
            for n, kind in enumerate(kinds):
                grad[pl.ds(64 * b + n, 8, stride=8), :] = kind

    def mixing():
        weight = [faces[8 * k : 8 * (k + 1), :] for k in range(modes + 1)]
        for s, term in enumerate(terms):
            total = weight[0] * grad[8 * s : 8 * (s + 1), :]
            for k in range(modes):
                mix = None
                for step, square in ((1, term[k] + 1), (-1, term[k])):
                    near = term[:k] + (term[k] + step,) + term[k + 1 :]
                    if near not in position:
                        continue
                    at = position[near]
                    value = grad[8 * at : 8 * (at + 1), :]
                    if square > 1:
                        value = math.sqrt(square) * value
                    mix = value if mix is None else mix + value
                if mix is not None:
                    total = total + weight[k + 1] * mix
            flux[8 * s : 8 * (s + 1), :] = total
        for s in range(len(terms), rows):
            flux[8 * s : 8 * (s + 1), :] = zero8

    def divergence(i, after):
        for b in range(rows // 8):
            kind = [flux[pl.ds(64 * b + n, 8, stride=8), :] for n in range(7)]
            part = pl.ds(8 * b, 8)
            for c in range(2):
                down = jnp.where(lane8 > 0, pltpu.roll(kind[3 + c], 1, 1), kind[5 + c])
                after(c, part, kind[c] - kind[c + 1] + down - kind[3 + c])

    gradients(0)
    mixing()
    arrive(f_of, sf, qf)
    got = select(rf[:, 0].reshape(8 * PAD, LANES), rf[:, 1].reshape(8 * PAD, LANES), True)
    for c in range(2):
        forced[c] = column(got, c)[0:rows]

    def first(c, part, value):
        field[1, c, part, :] = forced[c, part, :] - value

    divergence(0, first)
    halo_start(1)
    prepare_back(0)

    gradients(1)
    send_back(0)
    mixing()

    def second(c, part, value):
        field[2, c, part, :] = value

    divergence(1, second)
    halo_start(2)
    prepare_back(1)

    send_back(1)
    gradients(2)
    mixing()
    sums = [zero8] * 5

    def third(c, part, value):
        field[3, c, part, :] = value
        r, w = field[1, c, part, :], field[2, c, part, :]
        for n, (a, b) in enumerate(((r, r), (r, w), (w, w), (r, value), (w, value))):
            sums[n] = sums[n] + a * b

    divergence(2, third)
    dots(0, sums)
    dot_a_start(0)
    prepare_back(2)
    send_back(2)
    dot_b_start(0)
    total = dot_total(0)
    rr, rw, ww, rv, wv = (total[n : n + 1] for n in range(5))
    alpha = rr / rw
    rr1 = rr - 2.0 * alpha * rw + alpha * alpha * ww
    rar = rw - alpha * (rv + ww) + alpha * alpha * wv
    cross = 2.0 * rw - alpha * (ww + rv)
    beta = rr1 / rr
    step = rr1 / (rar + beta * cross + beta * beta * rw)

    arrive(back_of, so, qo)

    for c in range(cols):
        r0, w, v = back[0, c, 0:slots], back[1, c, 0:slots], back[2, c, 0:slots]
        x = x_ref[pl.ds(c, slots, stride=cols), :]
        xo_ref[pl.ds(c, slots, stride=cols), :] = x + (alpha + step + step * beta) * r0 - (step * alpha) * w
        r1 = r0 - alpha * w
        ro_ref[pl.ds(c, slots, stride=cols), :] = r1 - step * (w - alpha * v + beta * w)

    sent(codes_of, sc, qc)
    sent(x_of, sx, qx)
    sent(f_of, sf, qf)
    sent(back_of, so, qo)
    coef_copy.wait_send()
    for i in range(3):
        halo_sent(i)
    whole(dot_a.at[0, pl.ds(0, 7)], sda, qda.at[0]).wait_send()
    whole(dot_b.at[0, pl.ds(0, 15)], sdb, qdb.at[0]).wait_send()


def per_device(forcing, start_guess, mean_field, mode_fields, multi_index, coupled_slot):
    slots, cols, lanes = forcing.shape
    modes = mode_fields.shape[0]
    terms = term_list(modes, DEGREE)
    rows = -(-len(terms) // 8) * 8
    full = rows + 16
    wide = rows
    codes = np.full((8, wide), -2.0, np.float32)
    codes[:, : len(terms)] = [code_of(t) for t in terms]
    cfg = dict(slots=slots, cols=cols, terms=terms, modes=modes, rows=rows, full=full)
    flat = pltpu.VMEM((slots * cols, lanes), F32)
    vmem = pl.BlockSpec(memory_space=pltpu.VMEM)
    hbm = pl.BlockSpec(memory_space=pltpu.HBM)
    dma, V = pltpu.SemaphoreType.DMA, pltpu.VMEM
    scratch = [
        V((slots * cols, lanes), F32),
        V((slots * cols, lanes), F32),
        V((cols, lanes), F32),
        V((modes, cols, lanes), F32),
        V((modes, slots), jnp.int32),
        V((8, wide), F32),
        dma((6,)),
        V((cols, PAD, lanes), F32),
        V((cols, PAD, lanes), F32),
        V((8, lanes), F32),
        V((2, 2, 16, lanes), F32),
        V((8, 2, PAD, lanes), F32),
        V((8, 2, PAD, lanes), F32),
        V((8, 8, lanes), F32),
        V((2, 16, lanes), F32),
        V((8 * PAD, wide), F32),
        V((4, 2, full, lanes), F32),
        V((2, rows, lanes), F32),
        V((3, 2, full, lanes), F32),
        V((8 * rows, lanes), F32),
        V((8 * rows, lanes), F32),
        V((128, lanes), F32),
        V((3, 8, 2, PAD, lanes), F32),
        V((3, cols, PAD, lanes), F32),
        V((1, 8, lanes), F32),
        V((1, 8, 8, lanes), F32),
        V((1, 8, lanes), F32),
        V((1, 16, 8, lanes), F32),
        dma,
        dma,
        dma,
        dma,
        dma((3, 2)),
        dma,
        dma,
        dma,
        dma,
        dma,
        dma,
        dma,
        dma((3, 2)),
        dma,
        dma((1,)),
        dma((1,)),
    ]
    x, r = pl.pallas_call(
        functools.partial(kernel, cfg),
        out_shape=(flat, flat),
        in_specs=[hbm] * 6,
        out_specs=(vmem, vmem),
        scratch_shapes=scratch,
        compiler_params=pltpu.CompilerParams(
            collective_id=0, has_side_effects=True, vmem_limit_bytes=60 * 2**20
        ),
    )(
        forcing.reshape(slots * cols, lanes),
        start_guess.reshape(slots * cols, lanes),
        mean_field,
        mode_fields,
        multi_index.T,
        jnp.asarray(codes),
    )
    return (x.reshape(slots, cols, lanes), r.reshape(slots, cols, lanes))


def solution(mesh):
    placed = (
        P("chaos", "space", None),
        P("chaos", "space", None),
        P("space", None),
        P(None, "space", None),
        P("chaos", None),
        P("chaos", None),
    )
    return jax.shard_map(
        per_device,
        mesh=mesh,
        in_specs=placed,
        out_specs=(P("chaos", "space", None), P("chaos", "space", None)),
        check_vma=False,
    )
```
